32 devices in a mesh: groups: 2 (over y), space: 8 (over z, x), vec: 2 (over core).
Axes of the slice: x: 2, y: 2, z: 4, core: 2. Of those that a mesh axis runs over, the one named last changes fastest.
Arguments:
- perturbation: float32 [8, 5, 64, 8, 128], P(('groups', 'vec'), None, 'space'), parts along dimension 0, may hold values from -6 to 6
- forcing: float32 [8, 5, 64, 8, 128], P(('groups', 'vec'), None, 'space'), parts along dimension 0, may hold values from -6 to 6
- frequency: float32 [8], P(('groups', 'vec')), parts along dimension 0, may hold values from 0.5 to 6
- base_flow: float32 [6, 5, 64, 8, 128], P('vec', None, 'space'), may hold values from -1 to 1.4, as said below
- phase_slot: int32 [6], replicated, may hold values from 0 to 5, each once
Outputs:
- response: float32 [8, 5, 64, 8, 128], P(('groups', 'vec'), None, 'space'), parts along dimension 0
The draws below stay inside these ranges and needn't reach their ends.
There are 2 independent parts, one for each index of `groups`. The reference program is written for one: setup_inputs(seed, part) draws one part's arguments, and reference() takes and returns one part's arrays. A program takes and returns all parts, laid end to end along the dimension named above; an argument that names none is the same for every part. Nothing has to cross between parts.
Inputs may be any that keep to these rules, and one draw needn't show every extreme that they name: `phase_slot`: each stored slot serves exactly one time step. `base_flow`: field 0 (density) lies in 0.7 to 1.3, field 4 (pressure) in 0.6 to 1.4, fields 1 to 3 are velocities.
All inputs are finite; a program needn't handle non-finite values.
Results may differ from the reference program's by a relative error of at most 0.00002.
Values sent between devices are 32-bit elements; how exact they have to be, the bound alone decides.
No kernel may reach another device: no remote copies, remote signals or barrier semaphores. Data moves between devices by JAX's collectives and lax.ppermute only.
A program may use at most 128 MiB of HBM per device.

```python
import math
import jax
import jax.numpy as jnp
from jax import lax

VECS = 4
NY = 8
NZ = 128
NX = 64
PHASES = 6


def draw_base_flow(key, part):
    keys = jax.random.split(key, 3)
    density = jax.random.uniform(keys[0], (PHASES, 1, NX, NY, NZ), jnp.float32, 0.7, 1.3)
    pressure = jax.random.uniform(keys[1], (PHASES, 1, NX, NY, NZ), jnp.float32, 0.6, 1.4)
    velocity = jnp.clip(0.4 * jax.random.normal(keys[2], (PHASES, 3, NX, NY, NZ), jnp.float32), -1.0, 1.0)
    return jnp.concatenate([density, velocity, pressure], axis=1)


def levels(stream_key, dims, shards, least, largest):
    gain, own = 1.0, jax.random.fold_in(stream_key, 6)
    for dim, shards_of in shards:
        steps = jnp.exp(jax.random.uniform(jax.random.fold_in(own, dim), (shards_of,), jnp.float32, least / len(shards), largest / len(shards)))
        gain = gain * jnp.repeat(steps, dims[dim] // shards_of).reshape([-1 if axis == dim else 1 for axis in range(len(dims))])
    return gain


def gaussian(key, shape, scale, most, cuts=(), kind=jnp.bfloat16):
    drawn = jax.random.normal(key, shape, jnp.float32) * scale
    if len(cuts) > 0:
        drawn = levels(key, shape, cuts, -0.22, 0.18) * drawn
    return jnp.clip(drawn, min=-most, max=most).astype(kind)


def setup_inputs(seed: int = 0, part: int = 0) -> dict:
    key_of = jax.random.split(jax.random.key(seed), 6)
    own_keys = jax.random.split(jax.random.fold_in(key_of[5], part), 6)
    return {
        "perturbation": gaussian(own_keys[0], (VECS, 5, NX, NY, NZ), 1.0, 6.0, ((0, 2), (2, 8)), jnp.float32),
        "forcing": gaussian(own_keys[1], (VECS, 5, NX, NY, NZ), 1.0, 6.0, ((0, 2), (2, 8)), jnp.float32),
        "frequency": jnp.clip(jnp.exp(math.log(6.0) - 2.4849066 * jax.random.uniform(own_keys[2], (VECS,), jnp.float32) ** levels(own_keys[2], (VECS,), ((0, 2),), -0.2, 0.2)), 0.5, 6.0),
        "base_flow": draw_base_flow(jax.random.fold_in(key_of[5], 71), part),
        "phase_slot": jax.random.permutation(key_of[4], PHASES).astype(jnp.int32),
    }


HEAT_RATIO = 1.4
VISCOSITY = 0.1
TIME_STEP = 0.4


def along_first(padded):
    return 0.5 * (padded[..., 2:, :, :] - padded[..., :-2, :, :])


def along_other(interior, axis_pos):
    return 0.5 * (jnp.roll(interior, -1, axis_pos) - jnp.roll(interior, 1, axis_pos))


def gradient(padded):
    interior = padded[..., 1:-1, :, :]
    return interior, (along_first(padded), along_other(interior, -2), along_other(interior, -1))


def laplacian(padded):
    interior = padded[..., 1:-1, :, :]
    summed = padded[..., 2:, :, :] + padded[..., :-2, :, :]
    summed = summed + jnp.roll(interior, -1, -2) + jnp.roll(interior, 1, -2)
    summed = summed + jnp.roll(interior, -1, -1) + jnp.roll(interior, 1, -1)
    return summed - 6.0 * interior


def base_parts(padded):
    density, d_density = gradient(padded[0])
    velocity, d_velocity = gradient(padded[1:4])
    pressure, d_pressure = gradient(padded[4])
    divergence = d_velocity[0][0] + d_velocity[1][1] + d_velocity[2][2]
    return (density, d_density, velocity, d_velocity, pressure, d_pressure, divergence)


def tendency(padded, base_terms, forcing, frequency, moment):
    density, d_density, velocity, d_velocity, pressure, d_pressure, divergence = base_terms
    interior, d_state = gradient(padded)
    lap_velocity = laplacian(padded[:, 1:4])
    pert_density = interior[:, 0]
    pert_velocity = interior[:, 1:4]
    pert_pressure = interior[:, 4]
    pert_divergence = d_state[0][:, 1] + d_state[1][:, 2] + d_state[2][:, 3]
    carried = velocity[0] * d_state[0] + velocity[1] * d_state[1] + velocity[2] * d_state[2]
    onto_density = pert_velocity[:, 0] * d_density[0] + pert_velocity[:, 1] * d_density[1] + pert_velocity[:, 2] * d_density[2]
    onto_velocity = pert_velocity[:, 0:1] * d_velocity[0] + pert_velocity[:, 1:2] * d_velocity[1] + pert_velocity[:, 2:3] * d_velocity[2]
    onto_pressure = pert_velocity[:, 0] * d_pressure[0] + pert_velocity[:, 1] * d_pressure[1] + pert_velocity[:, 2] * d_pressure[2]
    grad_pert_pressure = jnp.stack([d_state[0][:, 4], d_state[1][:, 4], d_state[2][:, 4]], axis=1)
    grad_base_pressure = jnp.stack(d_pressure, axis=0)
    rate_density = -(carried[:, 0] + onto_density) - density * pert_divergence - pert_density * divergence
    rate_velocity = (-(carried[:, 1:4] + onto_velocity) - grad_pert_pressure / density
                     + pert_density[:, None] * grad_base_pressure / (density * density)
                     + VISCOSITY * lap_velocity)
    rate_pressure = -(carried[:, 4] + onto_pressure) - HEAT_RATIO * (pressure * pert_divergence + pert_pressure * divergence)
    driven = jnp.cos(frequency * moment)[:, None, None, None, None]
    joined = jnp.concatenate([rate_density[:, None], rate_velocity, rate_pressure[:, None]], axis=1)
    return joined + forcing * driven


def wrapped(field):
    return jnp.concatenate([field[..., -1:, :, :], field, field[..., :1, :, :]], axis=-3)


def reference(perturbation, forcing, frequency, base_flow, phase_slot):
    current = perturbation
    half_step = 0.5 * TIME_STEP
    for step_index in range(PHASES):
        base_tile = lax.dynamic_index_in_dim(base_flow, phase_slot[step_index].astype(jnp.int32), 0, keepdims=False)
        base_terms = base_parts(wrapped(base_tile))
        begin_time = step_index * TIME_STEP

        def advance(members):
            vector, driving, rate_freq = members
            vector = vector[None]
            driving = driving[None]
            rate_freq = rate_freq[None]
            section_one = tendency(wrapped(vector), base_terms, driving, rate_freq, begin_time)
            section_two = tendency(wrapped(vector + half_step * section_one), base_terms, driving, rate_freq, begin_time + half_step)
            section_three = tendency(wrapped(vector + half_step * section_two), base_terms, driving, rate_freq, begin_time + half_step)
            section_four = tendency(wrapped(vector + TIME_STEP * section_three), base_terms, driving, rate_freq, begin_time + TIME_STEP)
            updated = vector + TIME_STEP / 6.0 * (section_one + 2.0 * section_two + 2.0 * section_three + section_four)
            return updated[0]

        current = lax.map(advance, (current, forcing, frequency))
    return current
```

```python
import functools

import jax
import jax.numpy as jnp
from jax import lax
from jax.experimental import pallas as pl
from jax.experimental.pallas import tpu as pltpu
from jax.sharding import PartitionSpec as P

HEAT_RATIO = 1.4
VISCOSITY = 0.1
TIME_STEP = 0.4
FIELDS = 5
TERMS = 26
STAGES = 4
UNROLL = 2


VMEM = pl.BlockSpec(memory_space=pltpu.VMEM)
SMEM = pl.BlockSpec(memory_space=pltpu.SMEM)


def copy_planes(pairs):
    for dst, value in pairs:
        dst[...] = value


def pack_kernel(width, who, pert, force, base, swap_out, own_out, other_out):
    mine = who[0]
    other = 1 - mine
    tile = pert.shape[2]
    start = mine * (tile - width)
    edge = pl.ds(start, width)
    f = FIELDS
    swap_out[0:f] = pert[other]
    swap_out[f : 2 * f] = force[other]
    own_out[0:f] = pert[mine, :, edge]
    own_out[f : 2 * f] = force[mine, :, edge]
    other_out[0:f] = pert[other, :, edge]
    other_out[f : 2 * f] = force[other, :, edge]
    for slot in range(base.shape[0]):
        lo = (2 + slot) * f
        swap_out[lo : lo + f] = base[slot]
        own_out[lo : lo + f] = base[slot, :, edge]
        other_out[lo : lo + f] = base[slot, :, edge]


def assemble_kernel(width, who, pert, force, base, swap_in, own_in, other_in, state_out, force_out, base_out):
    mine = who[0]
    tile = pert.shape[2]
    f = FIELDS
    here = pl.ds(width + mine * tile, tile)
    there = pl.ds(width + (1 - mine) * tile, tile)
    far = width + 2 * tile
    own_at = pl.ds((1 - mine) * far, width)
    other_at = pl.ds(mine * far, width)
    state_out[:, here] = pert[mine]
    state_out[:, there] = swap_in[0:f]
    state_out[:, own_at] = own_in[0:f]
    state_out[:, other_at] = other_in[0:f]
    force_out[:, here] = force[mine]
    force_out[:, there] = swap_in[f : 2 * f]
    force_out[:, own_at] = own_in[f : 2 * f]
    force_out[:, other_at] = other_in[f : 2 * f]
    for slot in range(base.shape[0]):
        lo = slot * f
        base_out[lo : lo + f, here] = base[slot]
        base_out[lo : lo + f, there] = swap_in[2 * f + lo : 3 * f + lo]
        base_out[lo : lo + f, own_at] = own_in[2 * f + lo : 3 * f + lo]
        base_out[lo : lo + f, other_at] = other_in[2 * f + lo : 3 * f + lo]


def neighbours(ref, field, at, count):
    block = ref[field, pl.ds(at - 1, count + 2)]
    centre = block[1 : count + 1]
    return (
        centre,
        (block[2:], block[:count]),
        (pltpu.roll(centre, centre.shape[1] - 1, 1), pltpu.roll(centre, 1, 1)),
        (pltpu.roll(centre, centre.shape[2] - 1, 2), pltpu.roll(centre, 1, 2)),
    )


def base_terms(base, terms, at, count):
    centre, diff = [], []
    for field in range(FIELDS):
        mid, along_x, along_y, along_z = neighbours(base, field, at, count)
        centre.append(mid)
        diff.append([up - down for up, down in (along_x, along_y, along_z)])
    density, pressure = centre[0], centre[4]
    inverse = 1.0 / density
    square = 0.5 * inverse * inverse
    divergence = diff[1][0] + diff[2][1] + diff[3][2]
    out = [-0.5 * centre[1 + j] for j in range(3)]
    out += [-0.5 * diff[0][j] for j in range(3)]
    out += [-0.5 * density, -0.5 * divergence]
    for j in range(3):
        for k in range(3):
            slope = -0.5 * diff[1 + k][j]
            out.append(slope - 6.0 * VISCOSITY if j == k else slope)
    out += [-0.5 * inverse]
    out += [diff[4][k] * square for k in range(3)]
    out += [-0.5 * diff[4][j] for j in range(3)]
    out += [-0.5 * HEAT_RATIO * pressure, -0.5 * HEAT_RATIO * divergence]
    for index, value in enumerate(out):
        terms[index, pl.ds(at, count)] = value


def rates(state, terms, force, wave, at, count):
    here = pl.ds(at, count)
    centre, diff, around = [], [], []
    for field in range(FIELDS):
        mid, along_x, along_y, along_z = neighbours(state, field, at, count)
        centre.append(mid)
        diff.append([up - down for up, down in (along_x, along_y, along_z)])
        if 1 <= field <= 3:
            around.append((along_x[0] + along_x[1]) + (along_y[0] + along_y[1]) + (along_z[0] + along_z[1]))
    term = lambda index: terms[index, here]
    speed = [term(j) for j in range(3)]
    spread = diff[1][0] + diff[2][1] + diff[3][2]

    def carried(field, first, stride):
        total = force[field, here] * wave
        for j in range(3):
            total = total + (speed[j] * diff[field][j] + centre[1 + j] * term(first + stride * j))
        return total

    out = [carried(0, 3, 1) + (term(6) * spread + centre[0] * term(7))]
    inverse = term(17)
    for k in range(3):
        pull = inverse * diff[4][k] + centre[0] * term(18 + k)
        out.append(carried(1 + k, 8 + k, 3) + (pull + VISCOSITY * around[k]))
    out.append(carried(4, 21, 1) + (term(24) * spread + centre[4] * term(25)))
    return out


def over_planes(first, last, body):
    count = last - first
    whole = count // UNROLL

    def step(index, carry):
        body(first + index * UNROLL, UNROLL)
        return carry

    lax.fori_loop(0, whole, step, 0)
    if count % UNROLL:
        body(first + whole * UNROLL, count % UNROLL)


def one_step(inset, state, force, terms, waves, second, third, fourth):
    planes = state.shape[1]

    def stage(number, source, size, wave, target):
        def body(at, count):
            here = pl.ds(at, count)
            for field, rate in enumerate(rates(source, terms, force, wave, at, count)):
                target[field, here] = state[field, here] + size * rate

        over_planes(inset + number, planes - inset - number, body)

    stage(1, state, 0.5 * TIME_STEP, waves[0][None], second)
    stage(2, second, 0.5 * TIME_STEP, waves[1][None], third)
    stage(3, third, TIME_STEP, waves[1][None], fourth)

    def body(at, count):
        here = pl.ds(at, count)
        for field, rate in enumerate(rates(fourth, terms, force, waves[2][None], at, count)):
            mixed = second[field, here] + fourth[field, here] + 2.0 * third[field, here] - state[field, here]
            state[field, here] = mixed * (1.0 / 3.0) + (TIME_STEP / 6.0) * rate

    over_planes(inset + STAGES, planes - inset - STAGES, body)


def fetch_base(slot, who, base_here, base_there, base):
    local = base_here.shape[0] // FIELDS
    lo = lax.rem(slot, local) * FIELDS
    held = lax.div(slot, local) == who[1]

    @pl.when(held)
    def _():
        base[...] = base_here[pl.ds(lo, FIELDS)]

    @pl.when(jnp.logical_not(held))
    def _():
        base[...] = base_there[pl.ds(lo, FIELDS)]


def advance_kernel(first_step, width, ends, who, phase_slot, waves, force, base_here, base_there, *refs):
    first, last = ends
    if first:
        (state_in,), refs = refs[:1], refs[1:]
    else:
        (slab_in, left_in, right_in), refs = refs[:3], refs[3:]
    outs, (state, base, terms, second, third, fourth) = refs[:-6], refs[-6:]
    planes = state.shape[1]
    if first:
        state[...] = state_in[...]
    else:
        state[:, 0:width] = left_in[...]
        state[:, width : planes - width] = slab_in[...]
        state[:, planes - width :] = right_in[...]
    for index in range(width // STAGES):
        inset = STAGES * index
        fetch_base(phase_slot[first_step + index], who, base_here, base_there, base)
        over_planes(inset + 1, planes - inset - 1, functools.partial(base_terms, base, terms))
        wave = [waves[3 * index + which] for which in range(3)]
        one_step(inset, state, force, terms, wave, second, third, fourth)
    if last:
        keep, give = outs
        tile = keep.shape[1]
        mine = who[0]
        keep[...] = state[:, pl.ds(width + mine * tile, tile)]
        give[...] = state[:, pl.ds(width + (1 - mine) * tile, tile)]
    else:
        slab, left, right = outs
        slab[...] = state[:, width : planes - width]
        left[...] = state[:, width : 2 * width]
        right[...] = state[:, planes - 2 * width : planes - width]


def advance(first_step, width, ends, who, phase_slot, waves, force, base_here, base_there, carried):
    planes = force.shape[1]
    rows, lanes = force.shape[2:]
    block = lambda *lead: jax.ShapeDtypeStruct((*lead, rows, lanes), jnp.float32)
    slab = planes - 2 * width
    if ends[1]:
        outs = [block(FIELDS, slab // 2)] * 2
    else:
        outs = [block(FIELDS, slab), block(FIELDS, width), block(FIELDS, width)]
    scratch = lambda lead: pltpu.VMEM((lead, planes, rows, lanes), jnp.float32)
    return pl.pallas_call(
        functools.partial(advance_kernel, first_step, width, ends),
        out_shape=outs,
        in_specs=[SMEM, SMEM] + [VMEM] * (4 + len(carried)),
        out_specs=[VMEM] * len(outs),
        scratch_shapes=[scratch(FIELDS), scratch(FIELDS), scratch(TERMS)] + [scratch(FIELDS)] * 3,
        compiler_params=pltpu.CompilerParams(vmem_limit_bytes=32 << 20),
        name="advance",
    )(who, phase_slot, waves, force, base_here, base_there, *carried)


def per_device(width, perturbation, forcing, frequency, base_flow, phase_slot):
    _, _, tile, rows, lanes = perturbation.shape
    slots = base_flow.shape[0]
    count = lax.axis_size("space")
    steps = phase_slot.shape[0]
    place = lax.axis_index("space")
    mine = lax.rem(place, 2)
    who = jnp.stack([mine, lax.axis_index("vec")]).astype(jnp.int32)
    block = lambda *lead: jax.ShapeDtypeStruct((*lead, rows, lanes), jnp.float32)

    swap = [(i, i ^ 1) for i in range(count)]
    own = [(i, (i + 2 * (1 if i % 2 else -1)) % count) for i in range(count)]
    other = [(i, (i + (1 if i % 2 else -1)) % count) for i in range(count)]
    ahead = [(i, (i + 2) % count) for i in range(count)]
    behind = [(i, (i - 2) % count) for i in range(count)]
    core = [(0, 1), (1, 0)]

    lead = FIELDS * (2 + slots)
    swap_out, own_out, other_out = pl.pallas_call(
        functools.partial(pack_kernel, width),
        out_shape=[block(lead, tile), block(lead, width), block(lead, width)],
        in_specs=[SMEM] + [VMEM] * 3,
        out_specs=[VMEM] * 3,
        name="pack",
    )(who, perturbation, forcing, base_flow)
    swap_in = lax.ppermute(swap_out, "space", swap)
    own_in = lax.ppermute(own_out, "space", own)
    other_in = lax.ppermute(other_out, "space", other)

    planes = 2 * (tile + width)
    state, force, base_here = pl.pallas_call(
        functools.partial(assemble_kernel, width),
        out_shape=[block(FIELDS, planes), block(FIELDS, planes), block(FIELDS * slots, planes)],
        in_specs=[SMEM] + [VMEM] * 6,
        out_specs=[VMEM] * 3,
        name="assemble",
    )(who, perturbation, forcing, base_flow, swap_in, own_in, other_in)
    base_there = lax.ppermute(base_here, "vec", core)

    moments = jnp.array(
        [step * TIME_STEP + part for step in range(steps) for part in (0.0, 0.5 * TIME_STEP, TIME_STEP)],
        jnp.float32,
    )
    tuned = lax.dynamic_index_in_dim(frequency, mine, 0, keepdims=False)
    waves = jnp.broadcast_to(jnp.cos(tuned * moments)[:, None, None], (3 * steps, rows, lanes))

    per_round = width // STAGES
    carried = (state,)
    for first_step in range(0, steps, per_round):
        ends = (first_step == 0, first_step + per_round == steps)
        part = waves[3 * first_step : 3 * (first_step + per_round)]
        outs = advance(first_step, width, ends, who, phase_slot, part, force, base_here, base_there, carried)
        if not ends[1]:
            slab, left, right = outs
            carried = (slab, lax.ppermute(right, "space", ahead), lax.ppermute(left, "space", behind))
    keep, give = outs
    given = lax.ppermute(give, "space", swap)
    low, high = jnp.where(mine == 0, keep, given), jnp.where(mine == 0, given, keep)
    return jnp.stack([low, high])


def solution(mesh):
    return jax.shard_map(
        functools.partial(per_device, STAGES),
        mesh=mesh,
        in_specs=(
            P(("groups", "vec"), None, "space", None, None),
            P(("groups", "vec"), None, "space", None, None),
            P(("groups", "vec")),
            P("vec", None, "space", None, None),
            P(),
        ),
        out_specs=P(("groups", "vec"), None, "space", None, None),
        check_vma=False,
    )
```

```python
import functools

import jax
import jax.numpy as jnp
from jax import lax
from jax.experimental import pallas as pl
from jax.experimental.pallas import tpu as pltpu
from jax.sharding import PartitionSpec as P

HEAT_RATIO = 1.4
VISCOSITY = 0.1
TIME_STEP = 0.4
FIELDS = 5
TERMS = 26
STAGES = 4
UNROLL = 22


VMEM = pl.BlockSpec(memory_space=pltpu.VMEM)
SMEM = pl.BlockSpec(memory_space=pltpu.SMEM)


def copy_planes(pairs):
    for dst, value in pairs:
        dst[...] = value


def pack_kernel(width, who, pert, force, base, swap_out, own_out, other_out):
    mine = who[0]
    other = 1 - mine
    tile = pert.shape[2]
    start = mine * (tile - width)
    edge = pl.ds(start, width)
    f = FIELDS
    swap_out[0:f] = pert[other]
    swap_out[f : 2 * f] = force[other]
    own_out[0:f] = pert[mine, :, edge]
    own_out[f : 2 * f] = force[mine, :, edge]
    other_out[0:f] = pert[other, :, edge]
    other_out[f : 2 * f] = force[other, :, edge]
    for slot in range(base.shape[0]):
        lo = (2 + slot) * f
        swap_out[lo : lo + f] = base[slot]
        own_out[lo : lo + f] = base[slot, :, edge]
        other_out[lo : lo + f] = base[slot, :, edge]


def assemble_kernel(width, who, pert, force, base, swap_in, own_in, other_in, state_out, force_out, base_out):
    mine = who[0]
    tile = pert.shape[2]
    f = FIELDS
    here = pl.ds(width + mine * tile, tile)
    there = pl.ds(width + (1 - mine) * tile, tile)
    far = width + 2 * tile
    own_at = pl.ds((1 - mine) * far, width)
    other_at = pl.ds(mine * far, width)
    state_out[:, here] = pert[mine]
    state_out[:, there] = swap_in[0:f]
    state_out[:, own_at] = own_in[0:f]
    state_out[:, other_at] = other_in[0:f]
    force_out[:, here] = force[mine]
    force_out[:, there] = swap_in[f : 2 * f]
    force_out[:, own_at] = own_in[f : 2 * f]
    force_out[:, other_at] = other_in[f : 2 * f]
    for slot in range(base.shape[0]):
        lo = slot * f
        base_out[lo : lo + f, here] = base[slot]
        base_out[lo : lo + f, there] = swap_in[2 * f + lo : 3 * f + lo]
        base_out[lo : lo + f, own_at] = own_in[2 * f + lo : 3 * f + lo]
        base_out[lo : lo + f, other_at] = other_in[2 * f + lo : 3 * f + lo]


def neighbours(ref, field, at, count):
    block = ref[field, pl.ds(at - 1, count + 2)]
    centre = block[1 : count + 1]
    return (
        centre,
        (block[2:], block[:count]),
        (pltpu.roll(centre, centre.shape[1] - 1, 1), pltpu.roll(centre, 1, 1)),
        (pltpu.roll(centre, centre.shape[2] - 1, 2), pltpu.roll(centre, 1, 2)),
    )


def base_terms(base, terms, at, count):
    centre, diff = [], []
    for field in range(FIELDS):
        mid, along_x, along_y, along_z = neighbours(base, field, at, count)
        centre.append(mid)
        diff.append([up - down for up, down in (along_x, along_y, along_z)])
    density, pressure = centre[0], centre[4]
    inverse = 1.0 / density
    square = 0.5 * inverse * inverse
    divergence = diff[1][0] + diff[2][1] + diff[3][2]
    out = [-0.5 * centre[1 + j] for j in range(3)]
    out += [-0.5 * diff[0][j] for j in range(3)]
    out += [-0.5 * density, -0.5 * divergence]
    for j in range(3):
        for k in range(3):
            slope = -0.5 * diff[1 + k][j]
            out.append(slope - 6.0 * VISCOSITY if j == k else slope)
    out += [-0.5 * inverse]
    out += [diff[4][k] * square for k in range(3)]
    out += [-0.5 * diff[4][j] for j in range(3)]
    out += [-0.5 * HEAT_RATIO * pressure, -0.5 * HEAT_RATIO * divergence]
    for index, value in enumerate(out):
        terms[index, pl.ds(at, count)] = value


def rates(state, terms, force, wave, at, count):
    here = pl.ds(at, count)
    centre, diff, around = [], [], []
    for field in range(FIELDS):
        mid, along_x, along_y, along_z = neighbours(state, field, at, count)
        centre.append(mid)
        diff.append([up - down for up, down in (along_x, along_y, along_z)])
        if 1 <= field <= 3:
            around.append((along_x[0] + along_x[1]) + (along_y[0] + along_y[1]) + (along_z[0] + along_z[1]))
    term = lambda index: terms[index, here]
    speed = [term(j) for j in range(3)]
    spread = diff[1][0] + diff[2][1] + diff[3][2]

    def carried(field, first, stride):
        total = force[field, here] * wave
        for j in range(3):
            total = total + (speed[j] * diff[field][j] + centre[1 + j] * term(first + stride * j))
        return total

    out = [carried(0, 3, 1) + (term(6) * spread + centre[0] * term(7))]
    inverse = term(17)
    for k in range(3):
        pull = inverse * diff[4][k] + centre[0] * term(18 + k)
        out.append(carried(1 + k, 8 + k, 3) + (pull + VISCOSITY * around[k]))
    out.append(carried(4, 21, 1) + (term(24) * spread + centre[4] * term(25)))
    return out


def over_planes(first, last, body):
    count = last - first
    whole = count // UNROLL

    def step(index, carry):
        body(first + index * UNROLL, UNROLL)
        return carry

    lax.fori_loop(0, whole, step, 0)
    if count % UNROLL:
        body(first + whole * UNROLL, count % UNROLL)


def one_step(inset, state, force, terms, waves, second, third, fourth):
    planes = state.shape[1]

    def stage(number, source, size, wave, target):
        def body(at, count):
            here = pl.ds(at, count)
            for field, rate in enumerate(rates(source, terms, force, wave, at, count)):
                target[field, here] = state[field, here] + size * rate

        over_planes(inset + number, planes - inset - number, body)

    stage(1, state, 0.5 * TIME_STEP, waves[0][None], second)
    stage(2, second, 0.5 * TIME_STEP, waves[1][None], third)
    stage(3, third, TIME_STEP, waves[1][None], fourth)

    def body(at, count):
        here = pl.ds(at, count)
        for field, rate in enumerate(rates(fourth, terms, force, waves[2][None], at, count)):
            mixed = second[field, here] + fourth[field, here] + 2.0 * third[field, here] - state[field, here]
            state[field, here] = mixed * (1.0 / 3.0) + (TIME_STEP / 6.0) * rate

    over_planes(inset + STAGES, planes - inset - STAGES, body)


def fetch_base(slot, who, base_here, base_there, base):
    local = base_here.shape[0] // FIELDS
    lo = lax.rem(slot, local) * FIELDS
    held = lax.div(slot, local) == who[1]

    @pl.when(held)
    def _():
        base[...] = base_here[pl.ds(lo, FIELDS)]

    @pl.when(jnp.logical_not(held))
    def _():
        base[...] = base_there[pl.ds(lo, FIELDS)]


def advance_kernel(first_step, width, ends, who, phase_slot, waves, force, base_here, base_there, *refs):
    first, last = ends
    if first:
        (state_in,), refs = refs[:1], refs[1:]
    else:
        (slab_in, left_in, right_in), refs = refs[:3], refs[3:]
    outs, (state, base, terms, second, third, fourth) = refs[:-6], refs[-6:]
    planes = state.shape[1]
    if first:
        state[...] = state_in[...]
    else:
        state[:, 0:width] = left_in[...]
        state[:, width : planes - width] = slab_in[...]
        state[:, planes - width :] = right_in[...]
    for index in range(width // STAGES):
        inset = STAGES * index
        fetch_base(phase_slot[first_step + index], who, base_here, base_there, base)
        over_planes(inset + 1, planes - inset - 1, functools.partial(base_terms, base, terms))
        wave = [waves[3 * index + which] for which in range(3)]
        one_step(inset, state, force, terms, wave, second, third, fourth)
    if last:
        keep, give = outs
        tile = keep.shape[1]
        mine = who[0]
        keep[...] = state[:, pl.ds(width + mine * tile, tile)]
        give[...] = state[:, pl.ds(width + (1 - mine) * tile, tile)]
    else:
        slab, left, right = outs
        slab[...] = state[:, width : planes - width]
        left[...] = state[:, width : 2 * width]
        right[...] = state[:, planes - 2 * width : planes - width]


def advance(first_step, width, ends, who, phase_slot, waves, force, base_here, base_there, carried):
    planes = force.shape[1]
    rows, lanes = force.shape[2:]
    block = lambda *lead: jax.ShapeDtypeStruct((*lead, rows, lanes), jnp.float32)
    slab = planes - 2 * width
    if ends[1]:
        outs = [block(FIELDS, slab // 2)] * 2
    else:
        outs = [block(FIELDS, slab), block(FIELDS, width), block(FIELDS, width)]
    scratch = lambda lead: pltpu.VMEM((lead, planes, rows, lanes), jnp.float32)
    return pl.pallas_call(
        functools.partial(advance_kernel, first_step, width, ends),
        out_shape=outs,
        in_specs=[SMEM, SMEM] + [VMEM] * (4 + len(carried)),
        out_specs=[VMEM] * len(outs),
        scratch_shapes=[scratch(FIELDS), scratch(FIELDS), scratch(TERMS)] + [scratch(FIELDS)] * 3,
        compiler_params=pltpu.CompilerParams(vmem_limit_bytes=9 << 20),
        name="advance",
    )(who, phase_slot, waves, force, base_here, base_there, *carried)


def per_device(width, perturbation, forcing, frequency, base_flow, phase_slot):
    _, _, tile, rows, lanes = perturbation.shape
    slots = base_flow.shape[0]
    count = lax.axis_size("space")
    steps = phase_slot.shape[0]
    place = lax.axis_index("space")
    mine = lax.rem(place, 2)
    who = jnp.stack([mine, lax.axis_index("vec")]).astype(jnp.int32)
    block = lambda *lead: jax.ShapeDtypeStruct((*lead, rows, lanes), jnp.float32)

    swap = [(i, i ^ 1) for i in range(count)]
    own = [(i, (i + 2 * (1 if i % 2 else -1)) % count) for i in range(count)]
    other = [(i, (i + (1 if i % 2 else -1)) % count) for i in range(count)]
    ahead = [(i, (i + 2) % count) for i in range(count)]
    behind = [(i, (i - 2) % count) for i in range(count)]
    core = [(0, 1), (1, 0)]

    lead = FIELDS * (2 + slots)
    swap_out, own_out, other_out = pl.pallas_call(
        functools.partial(pack_kernel, width),
        out_shape=[block(lead, tile), block(lead, width), block(lead, width)],
        in_specs=[SMEM] + [VMEM] * 3,
        out_specs=[VMEM] * 3,
        compiler_params=pltpu.CompilerParams(vmem_limit_bytes=6 << 20),
        name="pack",
    )(who, perturbation, forcing, base_flow)
    swap_in = lax.ppermute(swap_out, "space", swap)
    own_in = lax.ppermute(own_out, "space", own)
    other_in = lax.ppermute(other_out, "space", other)

    planes = 2 * (tile + width)
    state, force, base_here = pl.pallas_call(
        functools.partial(assemble_kernel, width),
        out_shape=[block(FIELDS, planes), block(FIELDS, planes), block(FIELDS * slots, planes)],
        in_specs=[SMEM] + [VMEM] * 6,
        out_specs=[VMEM] * 3,
        compiler_params=pltpu.CompilerParams(vmem_limit_bytes=8 << 20),
        name="assemble",
    )(who, perturbation, forcing, base_flow, swap_in, own_in, other_in)
    base_there = lax.ppermute(base_here, "vec", core)

    moments = jnp.array(
        [step * TIME_STEP + part for step in range(steps) for part in (0.0, 0.5 * TIME_STEP, TIME_STEP)],
        jnp.float32,
    )
    tuned = lax.dynamic_index_in_dim(frequency, mine, 0, keepdims=False)
    waves = jnp.broadcast_to(jnp.cos(tuned * moments)[:, None, None], (3 * steps, rows, lanes))

    per_round = width // STAGES
    carried = (state,)
    for first_step in range(0, steps, per_round):
        ends = (first_step == 0, first_step + per_round == steps)
        part = waves[3 * first_step : 3 * (first_step + per_round)]
        outs = advance(first_step, width, ends, who, phase_slot, part, force, base_here, base_there, carried)
        if not ends[1]:
            slab, left, right = outs
            carried = (slab, lax.ppermute(right, "space", ahead), lax.ppermute(left, "space", behind))
    keep, give = outs
    given = lax.ppermute(give, "space", swap)
    low, high = jnp.where(mine == 0, keep, given), jnp.where(mine == 0, given, keep)
    return jnp.stack([low, high])


def solution(mesh):
    return jax.shard_map(
        functools.partial(per_device, STAGES),
        mesh=mesh,
        in_specs=(
            P(("groups", "vec"), None, "space", None, None),
            P(("groups", "vec"), None, "space", None, None),
            P(("groups", "vec")),
            P("vec", None, "space", None, None),
            P(),
        ),
        out_specs=P(("groups", "vec"), None, "space", None, None),
        check_vma=False,
    )
```

```python
import functools

import jax
import jax.numpy as jnp
from jax import lax
from jax.experimental import pallas as pl
from jax.experimental.pallas import tpu as pltpu
from jax.sharding import PartitionSpec as P

HEAT_RATIO = 1.4
VISCOSITY = 0.1
TIME_STEP = 0.4
FIELDS = 5
TERMS = 26
STAGES = 4


VMEM = pl.BlockSpec(memory_space=pltpu.VMEM)
SMEM = pl.BlockSpec(memory_space=pltpu.SMEM)
HBM = pl.BlockSpec(memory_space=pltpu.HBM)


def parity():
    return lax.rem(lax.axis_index("space"), 2)


def in_place(*arrays):
    return [pltpu.with_memory_space_constraint(array, pltpu.HBM) for array in arrays]


def after(values, *earlier):
    return lax.optimization_barrier((values, *earlier))[0]


def pallas(kernel, name, outs, in_specs, scratch=(), grant=4):
    return pl.pallas_call(
        kernel,
        out_shape=outs,
        in_specs=in_specs,
        out_specs=[VMEM] * len(outs),
        scratch_shapes=scratch,
        compiler_params=pltpu.CompilerParams(vmem_limit_bytes=grant << 20),
        name=name,
    )


def pack_kernel(sets, widths, reach, which, phase_slot, pert, force, base, base_peer, *refs):
    sends, kept, sem = refs[: 3 * len(which)], refs[3 * len(which) : -1], refs[-1]
    mine = parity()
    core = lax.axis_index("vec")
    other = 1 - mine
    tile = pert.shape[2]
    local = base.shape[0]
    waits = []

    def copy(source, target, at, count):
        into = target.at[:, pl.ds(at, count)]
        waits.append(pltpu.make_async_copy(source(), into, sem.at[len(waits)]))
        waits[-1].start()

    def copy_base(step, cells, target, at, count):
        into = target.at[:, pl.ds(at, count)]
        held = lax.div(phase_slot[step], local) == core
        row = lax.rem(phase_slot[step], local)
        first, second = [
            pltpu.make_async_copy(array.at[row, :, cells], into, sem.at[len(waits)]) for array in (base, base_peer)
        ]
        pl.when(held)(first.start)
        pl.when(jnp.logical_not(held))(second.start)
        waits.append(first)

    for index, chosen in enumerate(which):
        swap_out, own_out, other_out = sends[3 * index : 3 * index + 3]
        at_swap = at_edge = 0
        if chosen == 0:
            for array, width in ((pert, widths[0]), (force, reach)):
                edge = pl.ds(mine * (tile - width), width)
                copy(lambda: array.at[other], swap_out, at_swap, tile)
                copy(lambda: array.at[mine, :, edge], own_out, at_edge, width)
                copy(lambda: array.at[other, :, edge], other_out, at_edge, width)
                at_swap += tile
                at_edge += width
        for step in sets[chosen]:
            half, width = tile // 2, widths[step]
            copy_base(step, pl.ds(core * half, half), swap_out, at_swap, half)
            edge = pl.ds(mine * (tile - width) + core * (width // 2), width // 2)
            for target in (own_out, other_out):
                copy_base(step, edge, target, at_edge, width // 2)
            at_swap += half
            at_edge += width // 2
    if kept:
        held_state, held_base = kept
        copy(lambda: pert.at[mine], held_state, 0, tile)
        copy(lambda: force.at[mine], held_state, tile, tile)
        for step in range(held_base.shape[1] // tile):
            copy_base(step, pl.ds(0, tile), held_base, step * tile, tile)
    for wait in waits:
        wait.wait()


def waves_kernel(moments, frequency, waves):
    shape = waves.shape[1:]
    rows = lax.broadcasted_iota(jnp.int32, shape, 0)
    for first in range(0, len(moments), shape[0]):
        chunk = moments[first : first + shape[0]]
        angle = jnp.zeros(shape, jnp.float32)
        for row, moment in enumerate(chunk):
            angle = jnp.where(rows == row, moment, angle)
        wave = jnp.cos(frequency[parity()] * angle)
        for row in range(len(chunk)):
            waves[first + row] = jnp.broadcast_to(wave[row : row + 1], shape)


def neighbours(ref, field, at, count):
    block = ref[field, pl.ds(at - 1, count + 2)]
    centre = block[1 : count + 1]
    return (
        centre,
        (block[2:], block[:count]),
        (pltpu.roll(centre, centre.shape[1] - 1, 1), pltpu.roll(centre, 1, 1)),
        (pltpu.roll(centre, centre.shape[2] - 1, 2), pltpu.roll(centre, 1, 2)),
    )


def base_terms(base, terms, at, count):
    centre, diff = [], []
    for field in range(FIELDS):
        mid, along_x, along_y, along_z = neighbours(base, field, at, count)
        centre.append(mid)
        diff.append([up - down for up, down in (along_x, along_y, along_z)])
    density, pressure = centre[0], centre[4]
    inverse = 1.0 / density
    square = 0.5 * inverse * inverse
    divergence = diff[1][0] + diff[2][1] + diff[3][2]
    out = [-0.5 * centre[1 + j] for j in range(3)]
    out += [-0.5 * diff[0][j] for j in range(3)]
    out += [-0.5 * density, -0.5 * divergence]
    for j in range(3):
        for k in range(3):
            slope = -0.5 * diff[1 + k][j]
            out.append(slope - 6.0 * VISCOSITY if j == k else slope)
    out += [-0.5 * inverse]
    out += [diff[4][k] * square for k in range(3)]
    out += [-0.5 * diff[4][j] for j in range(3)]
    out += [-0.5 * HEAT_RATIO * pressure, -0.5 * HEAT_RATIO * divergence]
    for index, value in enumerate(out):
        terms[index, pl.ds(at, count)] = value


def terms_kernel(steps, widths, at_held, at_swap, at_edge, reach, held_base, *refs):
    mine_in, peer_in, outs, held = refs[:3], refs[3:6], refs[6:-1], refs[-1]
    mine = parity()
    core = lax.axis_index("vec")
    planes = held.shape[1]
    tile = planes // 2 - reach
    half = tile // 2
    at_peer_swap = at_peer_edge = 0
    for step, terms in zip(steps, outs):
        width = widths[step]
        held[:, pl.ds(reach + mine * tile, tile)] = held_base[:, at_held : at_held + tile]
        partner = reach + (1 - mine) * tile
        near, far = reach - width, reach + 2 * tile
        own_at = near + (1 - mine) * (far - near)
        other_at = near + mine * (far - near)
        for (swap_in, own_in, other_in), who, swap_lo, edge_lo in (
            (mine_in, core, at_swap, at_edge),
            (peer_in, 1 - core, at_peer_swap, at_peer_edge),
        ):
            edge = width // 2
            held[:, pl.ds(partner + who * half, half)] = swap_in[:, swap_lo : swap_lo + half]
            held[:, pl.ds(own_at + who * edge, edge)] = own_in[:, edge_lo : edge_lo + edge]
            held[:, pl.ds(other_at + who * edge, edge)] = other_in[:, edge_lo : edge_lo + edge]
        base_terms(held, terms, near + 1, planes - 2 * near - 2)
        at_held += tile
        at_swap, at_peer_swap = at_swap + half, at_peer_swap + half
        at_edge, at_peer_edge = at_edge + width // 2, at_peer_edge + width // 2


def rates(state, terms, force, wave, at, count):
    here = pl.ds(at, count)
    centre, diff, around = [], [], []
    for field in range(FIELDS):
        mid, along_x, along_y, along_z = neighbours(state, field, at, count)
        centre.append(mid)
        diff.append([up - down for up, down in (along_x, along_y, along_z)])
        if 1 <= field <= 3:
            around.append((along_x[0] + along_x[1]) + (along_y[0] + along_y[1]) + (along_z[0] + along_z[1]))
    term = lambda index: terms[index, here]
    speed = [term(j) for j in range(3)]
    spread = diff[1][0] + diff[2][1] + diff[3][2]

    def carried(field, first, stride):
        total = force[field, here] * wave
        for j in range(3):
            total = total + (speed[j] * diff[field][j] + centre[1 + j] * term(first + stride * j))
        return total

    out = [carried(0, 3, 1) + (term(6) * spread + centre[0] * term(7))]
    inverse = term(17)
    for k in range(3):
        pull = inverse * diff[4][k] + centre[0] * term(18 + k)
        out.append(carried(1 + k, 8 + k, 3) + (pull + VISCOSITY * around[k]))
    out.append(carried(4, 21, 1) + (term(24) * spread + centre[4] * term(25)))
    return out


def one_step(inset, state, force, terms, waves, second, third, fourth):
    planes = state.shape[1]

    def stage(number, source, size, wave, target):
        at, count = inset + number, planes - 2 * (inset + number)
        here = pl.ds(at, count)
        for field, rate in enumerate(rates(source, terms, force, wave[None], at, count)):
            target[field, here] = state[field, here] + size * rate

    stage(1, state, 0.5 * TIME_STEP, waves[0], second)
    stage(2, second, 0.5 * TIME_STEP, waves[1], third)
    stage(3, third, TIME_STEP, waves[1], fourth)
    at, count = inset + STAGES, planes - 2 * (inset + STAGES)
    here = pl.ds(at, count)
    for field, rate in enumerate(rates(fourth, terms, force, waves[2][None], at, count)):
        mixed = second[field, here] + fourth[field, here] + 2.0 * third[field, here] - state[field, here]
        state[field, here] = mixed * (1.0 / 3.0) + (TIME_STEP / 6.0) * rate


def advance_kernel(steps, widths, reach, first, last, next_width, waves, *refs):
    terms, refs = refs[: len(steps)], refs[len(steps) :]
    width = widths[steps[0]]
    state, second, third, fourth = refs[-4:]
    refs = refs[:-4]
    planes = state.shape[1]
    tile = planes // 2 - reach
    mine = parity()
    near, far = reach - width, reach + 2 * tile
    if first:
        held_state, swap_in, own_in, other_in, force, *outs = refs
        here, there = pl.ds(reach + mine * tile, tile), pl.ds(reach + (1 - mine) * tile, tile)
        state[:, here] = held_state[:, 0:tile]
        state[:, there] = swap_in[:, 0:tile]
        state[:, pl.ds(near + (1 - mine) * (far - near), width)] = own_in[:, 0:width]
        state[:, pl.ds(near + mine * (far - near), width)] = other_in[:, 0:width]
        force[:, here] = held_state[:, tile : 2 * tile]
        force[:, there] = swap_in[:, tile : 2 * tile]
        force[:, pl.ds((1 - mine) * far, reach)] = own_in[:, width : width + reach]
        force[:, pl.ds(mine * far, reach)] = other_in[:, width : width + reach]
    else:
        force, slab_in, left_in, right_in, *outs = refs
        state[:, near:reach] = left_in[...]
        state[:, reach:far] = slab_in[...]
        state[:, far : far + width] = right_in[...]
    for index, step in enumerate(steps):
        wave = [waves[3 * step + which] for which in range(3)]
        one_step(reach - widths[step], state, force, terms[index], wave, second, third, fourth)
    if last:
        keep, give = outs
        keep[...] = state[:, pl.ds(reach + mine * tile, tile)]
        give[...] = state[:, pl.ds(reach + (1 - mine) * tile, tile)]
    else:
        slab, left, right = outs
        slab[...] = state[:, reach:far]
        left[...] = state[:, reach : reach + next_width]
        right[...] = state[:, far - next_width : far]


def per_device(perturbation, forcing, frequency, base_flow, phase_slot):
    _, _, tile, rows, lanes = perturbation.shape
    count = lax.axis_size("space")
    steps = phase_slot.shape[0]
    block = lambda *lead: jax.ShapeDtypeStruct((*lead, rows, lanes), jnp.float32)
    scratch = lambda *lead: pltpu.VMEM((*lead, rows, lanes), jnp.float32)

    rounds = [list(range(start, min(start + 2, steps))) for start in range(0, steps, 2)]
    sets = [each for each in (rounds[0], sum(rounds[1:], [])) if each]
    widths = {step: STAGES * (each[-1] - step + 1) for each in rounds for step in each}
    reach = max(widths.values())
    planes = 2 * (tile + reach)

    swap = [(i, i ^ 1) for i in range(count)]
    own = [(i, (i + 2 * (1 if i % 2 else -1)) % count) for i in range(count)]
    other = [(i, (i + (1 if i % 2 else -1)) % count) for i in range(count)]
    ahead = [(i, (i + 2) % count) for i in range(count)]
    behind = [(i, (i - 2) % count) for i in range(count)]
    core = [(0, 1), (1, 0)]

    base_peer = lax.ppermute(base_flow, "vec", core)
    moments = [step * TIME_STEP + part for step in range(steps) for part in (0.0, 0.5 * TIME_STEP, TIME_STEP)]

    def pack(which, keep):
        sends, copies = [], 0
        for chosen in which:
            group, start = sets[chosen], chosen == 0
            swapped = len(group) * (tile // 2) + (2 * tile if start else 0)
            edges = sum(widths[step] // 2 for step in group) + (widths[0] + reach if start else 0)
            sends += [block(FIELDS, swapped), block(FIELDS, edges), block(FIELDS, edges)]
            copies += 3 * len(group) + (6 if start else 0)
        kept = [block(FIELDS, 2 * tile), block(FIELDS, steps * tile)] if keep else []
        return pallas(
            functools.partial(pack_kernel, sets, widths, reach, which),
            "pack",
            sends + kept,
            [SMEM] + [HBM] * 4,
            [pltpu.SemaphoreType.DMA((copies + (2 + steps if keep else 0),))],
        )(*in_place(phase_slot, perturbation, forcing, base_flow), base_peer)

    def exchange(packed):
        return [lax.ppermute(part, "space", perm) for part, perm in zip(packed, (swap, own, other))]

    def factors(which, arrived):
        group = sets[which]
        at_swap, at_edge = (2 * tile, widths[0] + reach) if which == 0 else (0, 0)
        crossed = [
            lax.ppermute(part[:, at:] if at else part, "vec", core)
            for part, at in zip(arrived, (at_swap, at_edge, at_edge))
        ]
        return pallas(
            functools.partial(terms_kernel, group, widths, group[0] * tile, at_swap, at_edge, reach),
            "terms",
            [block(TERMS, planes)] * len(group),
            [VMEM] * 7,
            [scratch(FIELDS, planes)],
            grant=2,
        )(held_base, *arrived, *crossed)

    def advance(which, operands):
        group = rounds[which]
        first, last = which == 0, which == len(rounds) - 1
        next_width = 0 if last else widths[rounds[which + 1][0]]
        if last:
            outs = [block(FIELDS, tile)] * 2
        else:
            outs = [block(FIELDS, 2 * tile), block(FIELDS, next_width), block(FIELDS, next_width)]
        if first:
            outs = [block(FIELDS, planes)] + outs
        return pallas(
            functools.partial(advance_kernel, group, widths, reach, first, last, next_width),
            "advance",
            outs,
            [VMEM] * (1 + len(operands)),
            [scratch(FIELDS, planes)] * 4,
            grant=8,
        )(waves, *operands)

    first = exchange(pack([0], False))
    *later, held_state, held_base = pack(range(1, len(sets)), True)
    (waves,) = pallas(functools.partial(waves_kernel, moments), "waves", [block(3 * steps)], [SMEM])(*in_place(frequency))
    packed = [None] + [later[3 * which : 3 * which + 3] for which in range(len(sets) - 1)]
    arrived = exchange(after(packed[1], first[1])) if len(sets) > 1 else None
    first, held_state, held_base, waves = lax.optimization_barrier((first, held_state, held_base, waves))
    terms = dict(zip(sets[0], factors(0, first)))
    force, *outs = advance(0, [*[terms[step] for step in rounds[0]], held_state, *first])
    for which in range(1, len(rounds)):
        slab, left, right = outs
        left_in = lax.ppermute(right, "space", ahead)
        right_in = lax.ppermute(left, "space", behind)
        if which < len(sets):
            arrived = after(arrived, slab)
            following = exchange(after(packed[which + 1], arrived)) if which + 1 < len(sets) else None
            terms |= zip(sets[which], factors(which, arrived))
            arrived = following
        outs = advance(which, [*[terms[step] for step in rounds[which]], force, slab, left_in, right_in])
    keep, give = outs
    given = lax.ppermute(give, "space", swap)
    mine = parity()
    low, high = jnp.where(mine == 0, keep, given), jnp.where(mine == 0, given, keep)
    return jnp.stack([low, high])


def solution(mesh):
    return jax.shard_map(
        per_device,
        mesh=mesh,
        in_specs=(
            P(("groups", "vec"), None, "space", None, None),
            P(("groups", "vec"), None, "space", None, None),
            P(("groups", "vec")),
            P("vec", None, "space", None, None),
            P(),
        ),
        out_specs=P(("groups", "vec"), None, "space", None, None),
        check_vma=False,
    )
```

```python
import functools

import jax
import jax.numpy as jnp
from jax import lax
from jax.experimental import pallas as pl
from jax.experimental.pallas import tpu as pltpu
from jax.sharding import PartitionSpec as P

HEAT_RATIO = 1.4
VISCOSITY = 0.1
TIME_STEP = 0.4
FIELDS = 5
TERMS = 26
STAGES = 4


VMEM = pl.BlockSpec(memory_space=pltpu.VMEM)
SMEM = pl.BlockSpec(memory_space=pltpu.SMEM)
HBM = pl.BlockSpec(memory_space=pltpu.HBM)


def parity():
    return lax.rem(lax.axis_index("space"), 2)


def in_place(*arrays):
    return [pltpu.with_memory_space_constraint(array, pltpu.HBM) for array in arrays]


def after(values, *earlier):
    return lax.optimization_barrier((values, *earlier))[0]


def pallas(kernel, name, outs, in_specs, scratch=(), grant=4):
    return pl.pallas_call(
        kernel,
        out_shape=outs,
        in_specs=in_specs,
        out_specs=[VMEM] * len(outs),
        scratch_shapes=scratch,
        compiler_params=pltpu.CompilerParams(vmem_limit_bytes=grant << 20),
        name=name,
    )


def pack_kernel(sets, widths, reach, which, phase_slot, pert, force, base, base_peer, *refs):
    count = sum(3 if chosen == 0 else 2 for chosen in which)
    sends, kept, sem = refs[:count], refs[count:-1], refs[-1]
    mine = parity()
    core = lax.axis_index("vec")
    other = 1 - mine
    tile = pert.shape[2]
    local = base.shape[0]
    waits = []

    def copy(source, target, at, count):
        into = target.at[:, pl.ds(at, count)]
        waits.append(pltpu.make_async_copy(source(), into, sem.at[len(waits)]))
        waits[-1].start()

    def copy_base(step, cells, target, at, count):
        into = target.at[:, pl.ds(at, count)]
        held = lax.div(phase_slot[step], local) == core
        row = lax.rem(phase_slot[step], local)
        first, second = [
            pltpu.make_async_copy(array.at[row, :, cells], into, sem.at[len(waits)]) for array in (base, base_peer)
        ]
        pl.when(held)(first.start)
        pl.when(jnp.logical_not(held))(second.start)
        waits.append(first)

    for chosen in which:
        if chosen == 0:
            swap_out, own_out, other_out, *sends = sends
        else:
            swap_out, other_out, *sends = sends
        at_swap = at_other = at_own = 0
        if chosen == 0:
            for array, width in ((pert, widths[0]), (force, reach)):
                edge = pl.ds(mine * (tile - width), width)
                copy(lambda: array.at[other], swap_out, at_swap, tile)
                copy(lambda: array.at[mine, :, edge], own_out, at_own, width)
                copy(lambda: array.at[other, :, edge], other_out, at_other, width)
                at_swap += tile
                at_own += width
                at_other += width
        half = tile // 2
        layers = lambda step: pl.ds(mine * (tile - widths[step]) + core * (widths[step] // 2), widths[step] // 2)
        for step in sets[chosen]:
            copy_base(step, pl.ds(core * half, half), swap_out, at_swap, half)
            copy_base(step, layers(step), other_out, at_other, widths[step] // 2)
            at_swap += half
            at_other += widths[step] // 2
        if chosen == 0:
            for step in sum(sets, []):
                copy_base(step, layers(step), own_out, at_own, widths[step] // 2)
                at_own += widths[step] // 2
    if kept:
        held_state, held_base = kept
        copy(lambda: pert.at[mine], held_state, 0, tile)
        copy(lambda: force.at[mine], held_state, tile, tile)
        for step in range(held_base.shape[1] // tile):
            copy_base(step, pl.ds(0, tile), held_base, step * tile, tile)
    for wait in waits:
        wait.wait()


def waves_kernel(moments, frequency, waves):
    shape = waves.shape[1:]
    rows = lax.broadcasted_iota(jnp.int32, shape, 0)
    for first in range(0, len(moments), shape[0]):
        chunk = moments[first : first + shape[0]]
        angle = jnp.zeros(shape, jnp.float32)
        for row, moment in enumerate(chunk):
            angle = jnp.where(rows == row, moment, angle)
        wave = jnp.cos(frequency[parity()] * angle)
        for row in range(len(chunk)):
            waves[first + row] = jnp.broadcast_to(wave[row : row + 1], shape)


def neighbours(ref, field, at, count):
    block = ref[field, pl.ds(at - 1, count + 2)]
    centre = block[1 : count + 1]
    return (
        centre,
        (block[2:], block[:count]),
        (pltpu.roll(centre, centre.shape[1] - 1, 1), pltpu.roll(centre, 1, 1)),
        (pltpu.roll(centre, centre.shape[2] - 1, 2), pltpu.roll(centre, 1, 2)),
    )


def base_terms(base, terms, at, count):
    centre, diff = [], []
    for field in range(FIELDS):
        mid, along_x, along_y, along_z = neighbours(base, field, at, count)
        centre.append(mid)
        diff.append([up - down for up, down in (along_x, along_y, along_z)])
    density, pressure = centre[0], centre[4]
    inverse = 1.0 / density
    square = 0.5 * inverse * inverse
    divergence = diff[1][0] + diff[2][1] + diff[3][2]
    out = [-0.5 * centre[1 + j] for j in range(3)]
    out += [-0.5 * diff[0][j] for j in range(3)]
    out += [-0.5 * density, -0.5 * divergence]
    for j in range(3):
        for k in range(3):
            slope = -0.5 * diff[1 + k][j]
            out.append(slope - 6.0 * VISCOSITY if j == k else slope)
    out += [-0.5 * inverse]
    out += [diff[4][k] * square for k in range(3)]
    out += [-0.5 * diff[4][j] for j in range(3)]
    out += [-0.5 * HEAT_RATIO * pressure, -0.5 * HEAT_RATIO * divergence]
    for index, value in enumerate(out):
        terms[index, pl.ds(at, count)] = value


def terms_kernel(steps, widths, at_held, starts, reach, held_base, *refs):
    mine_in, peer_in, outs, held = refs[:3], refs[3:6], refs[6:-1], refs[-1]
    mine = parity()
    core = lax.axis_index("vec")
    planes = held.shape[1]
    tile = planes // 2 - reach
    half = tile // 2
    starts = [list(starts), [0, 0, 0]]
    for step, terms in zip(steps, outs):
        width = widths[step]
        held[:, pl.ds(reach + mine * tile, tile)] = held_base[:, at_held : at_held + tile]
        partner = reach + (1 - mine) * tile
        near, far = reach - width, reach + 2 * tile
        own_at = near + (1 - mine) * (far - near)
        other_at = near + mine * (far - near)
        for (swap_in, own_in, other_in), who, start in zip((mine_in, peer_in), (core, 1 - core), starts):
            edge = width // 2
            at_swap, at_own, at_other = start
            held[:, pl.ds(partner + who * half, half)] = swap_in[:, at_swap : at_swap + half]
            held[:, pl.ds(own_at + who * edge, edge)] = own_in[:, at_own : at_own + edge]
            held[:, pl.ds(other_at + who * edge, edge)] = other_in[:, at_other : at_other + edge]
            start[:] = [at_swap + half, at_own + edge, at_other + edge]
        for at, count in singly([(near + 1, planes - 2 * near - 2)]):
            base_terms(held, terms, at, count)
        at_held += tile


def rates(state, terms, force, wave, at, count):
    here = pl.ds(at, count)
    centre, diff, around = [], [], []
    for field in range(FIELDS):
        mid, along_x, along_y, along_z = neighbours(state, field, at, count)
        centre.append(mid)
        diff.append([up - down for up, down in (along_x, along_y, along_z)])
        if 1 <= field <= 3:
            around.append((along_x[0] + along_x[1]) + (along_y[0] + along_y[1]) + (along_z[0] + along_z[1]))
    term = lambda index: terms[index, here]
    speed = [term(j) for j in range(3)]
    spread = diff[1][0] + diff[2][1] + diff[3][2]

    def carried(field, first, stride):
        total = force[field, here] * wave
        for j in range(3):
            total = total + (speed[j] * diff[field][j] + centre[1 + j] * term(first + stride * j))
        return total

    out = [carried(0, 3, 1) + (term(6) * spread + centre[0] * term(7))]
    inverse = term(17)
    for k in range(3):
        pull = inverse * diff[4][k] + centre[0] * term(18 + k)
        out.append(carried(1 + k, 8 + k, 3) + (pull + VISCOSITY * around[k]))
    out.append(carried(4, 21, 1) + (term(24) * spread + centre[4] * term(25)))
    return out


def singly(ranges):
    return [(at, 1) for first, count in ranges for at in range(first, first + count)]


def one_step(cover, depth, state, force, terms, waves, second, third, fourth):
    def stage(number, source, size, wave, target):
        for at, count in singly(cover(depth + number)):
            here = pl.ds(at, count)
            for field, rate in enumerate(rates(source, terms, force, wave[None], at, count)):
                target[field, here] = state[field, here] + size * rate

    stage(1, state, 0.5 * TIME_STEP, waves[0], second)
    stage(2, second, 0.5 * TIME_STEP, waves[1], third)
    stage(3, third, TIME_STEP, waves[1], fourth)
    for at, count in singly(cover(depth + STAGES)):
        here = pl.ds(at, count)
        for field, rate in enumerate(rates(fourth, terms, force, waves[2][None], at, count)):
            mixed = second[field, here] + fourth[field, here] + 2.0 * third[field, here] - state[field, here]
            state[field, here] = mixed * (1.0 / 3.0) + (TIME_STEP / 6.0) * rate


def several(steps, cover, waves, state, force, terms, *stages):
    for index, step in enumerate(steps):
        wave = [waves[3 * step + which] for which in range(3)]
        one_step(cover, STAGES * index, state, force, terms[index], wave, *stages)


def inner(reach, slab, depth):
    return [(reach + depth, slab - 2 * depth)] if slab > 2 * depth else []


def outer(reach, slab, width, depth):
    low, high = reach - width + depth, reach + slab + width - depth
    if not inner(reach, slab, depth):
        return [(low, high - low)]
    return [(low, width), (high - width, width)]


def interior_kernel(steps, reach, waves, *refs):
    terms, (force, slab, *refs) = refs[: len(steps)], refs[len(steps) :]
    outs, scratch = refs[:4], refs[4:]
    planes = slab.shape[1]
    scratch[0][:, reach : reach + planes] = slab[...]
    several(steps, functools.partial(inner, reach, planes), waves, scratch[0], force, terms, *scratch[1:])
    for index, (out, held) in enumerate(zip(outs, scratch)):
        out[:, index : planes - index] = held[:, reach + index : reach + planes - index]


def advance_kernel(steps, widths, reach, first, last, next_width, waves, *refs):
    terms, refs = refs[: len(steps)], refs[len(steps) :]
    width = widths[steps[0]]
    state, second, third, fourth = refs[-4:]
    refs = refs[:-4]
    planes = state.shape[1]
    tile = planes // 2 - reach
    mine = parity()
    near, far = reach - width, reach + 2 * tile
    if first:
        held_state, swap_in, own_in, other_in, force, *outs = refs
        here, there = pl.ds(reach + mine * tile, tile), pl.ds(reach + (1 - mine) * tile, tile)
        state[:, here] = held_state[:, 0:tile]
        state[:, there] = swap_in[:, 0:tile]
        state[:, pl.ds(near + (1 - mine) * (far - near), width)] = own_in[:, 0:width]
        state[:, pl.ds(near + mine * (far - near), width)] = other_in[:, 0:width]
        force[:, here] = held_state[:, tile : 2 * tile]
        force[:, there] = swap_in[:, tile : 2 * tile]
        force[:, pl.ds((1 - mine) * far, reach)] = own_in[:, width : width + reach]
        force[:, pl.ds(mine * far, reach)] = other_in[:, width : width + reach]
        cover = lambda depth: [(near + depth, planes - 2 * (near + depth))]
    else:
        force, left_in, right_in, *refs = refs
        begun, outs = refs[:4], refs[4:]
        for index, (source, held) in enumerate(zip(begun, (state, second, third, fourth))):
            held[:, reach + index : far - index] = source[:, index : 2 * tile - index]
        state[:, near:reach] = left_in[...]
        state[:, far : far + width] = right_in[...]
        cover = functools.partial(outer, reach, 2 * tile, width)
    several(steps, cover, waves, state, force, terms, second, third, fourth)
    if last:
        keep, give = outs
        keep[...] = state[:, pl.ds(reach + mine * tile, tile)]
        give[...] = state[:, pl.ds(reach + (1 - mine) * tile, tile)]
    else:
        slab, left, right = outs
        slab[...] = state[:, reach:far]
        left[...] = state[:, reach : reach + next_width]
        right[...] = state[:, far - next_width : far]


def per_device(perturbation, forcing, frequency, base_flow, phase_slot):
    _, _, tile, rows, lanes = perturbation.shape
    count = lax.axis_size("space")
    steps = phase_slot.shape[0]
    block = lambda *lead: jax.ShapeDtypeStruct((*lead, rows, lanes), jnp.float32)
    scratch = lambda *lead: pltpu.VMEM((*lead, rows, lanes), jnp.float32)

    rounds = [list(range(start, min(start + 2, steps))) for start in range(0, steps, 2)]
    sets = [each for each in (rounds[0], sum(rounds[1:], [])) if each]
    widths = {step: STAGES * (each[-1] - step + 1) for each in rounds for step in each}
    reach = max(widths.values())
    planes = 2 * (tile + reach)

    swap = [(i, i ^ 1) for i in range(count)]
    own = [(i, (i + 2 * (1 if i % 2 else -1)) % count) for i in range(count)]
    other = [(i, (i + (1 if i % 2 else -1)) % count) for i in range(count)]
    ahead = [(i, (i + 2) % count) for i in range(count)]
    behind = [(i, (i - 2) % count) for i in range(count)]
    core = [(0, 1), (1, 0)]

    base_peer = lax.ppermute(base_flow, "vec", core)
    moments = [step * TIME_STEP + part for step in range(steps) for part in (0.0, 0.5 * TIME_STEP, TIME_STEP)]

    def pack(which, keep):
        sends, copies = [], 0
        for chosen in which:
            group, start = sets[chosen], chosen == 0
            swapped = len(group) * (tile // 2) + (2 * tile if start else 0)
            edges = sum(widths[step] // 2 for step in group) + (widths[0] + reach if start else 0)
            every = sum(widths.values()) // 2 + widths[0] + reach
            sends += [block(FIELDS, swapped)] + ([block(FIELDS, every)] if start else []) + [block(FIELDS, edges)]
            copies += 2 * len(group) + (6 + steps if start else 0)
        kept = [block(FIELDS, 2 * tile), block(FIELDS, steps * tile)] if keep else []
        return pallas(
            functools.partial(pack_kernel, sets, widths, reach, which),
            "pack",
            sends + kept,
            [SMEM] + [HBM] * 4,
            [pltpu.SemaphoreType.DMA((copies + (2 + steps if keep else 0),))],
        )(*in_place(phase_slot, perturbation, forcing, base_flow), base_peer)

    def exchange(packed, perms):
        return [lax.ppermute(part, "space", perm) for part, perm in zip(packed, perms)]

    def factors(which, arrived):
        group = sets[which]
        edges = sum(widths[step] // 2 for step in group)
        starts = [2 * tile, widths[0] + reach, widths[0] + reach] if which == 0 else [0, 0, 0]
        if which > 0:
            starts[1] = widths[0] + reach + sum(widths[step] // 2 for each in sets[:which] for step in each)
        sizes = (len(group) * tile // 2, edges, edges)
        crossed = [
            lax.ppermute(part[:, at : at + size], "vec", core) for part, at, size in zip(arrived, starts, sizes)
        ]
        return pallas(
            functools.partial(terms_kernel, group, widths, group[0] * tile, starts, reach),
            "terms",
            [block(TERMS, planes)] * len(group),
            [VMEM] * 7,
            [scratch(FIELDS, planes)],
            grant=2,
        )(held_base, *arrived, *crossed)

    def advance(which, operands):
        group = rounds[which]
        first, last = which == 0, which == len(rounds) - 1
        next_width = 0 if last else widths[rounds[which + 1][0]]
        if last:
            outs = [block(FIELDS, tile)] * 2
        else:
            outs = [block(FIELDS, 2 * tile), block(FIELDS, next_width), block(FIELDS, next_width)]
        if first:
            outs = [block(FIELDS, planes)] + outs
        return pallas(
            functools.partial(advance_kernel, group, widths, reach, first, last, next_width),
            "advance",
            outs,
            [VMEM] * (1 + len(operands)),
            [scratch(FIELDS, planes)] * 4,
            grant=8,
        )(waves, *operands)

    first = exchange(pack([0], False), (swap, own, other))
    *later, held_state, held_base = pack(range(1, len(sets)), True)
    (waves,) = pallas(functools.partial(waves_kernel, moments), "waves", [block(3 * steps)], [SMEM])(*in_place(frequency))
    arrived = exchange(later, (swap, other))
    first, held_state, held_base, waves = lax.optimization_barrier((first, held_state, held_base, waves))
    terms = dict(zip(sets[0], factors(0, first)))
    force, *outs = advance(0, [*[terms[step] for step in rounds[0]], held_state, *first])
    for which in range(1, len(rounds)):
        slab, left, right = outs
        left_in = lax.ppermute(right, "space", ahead)
        right_in = lax.ppermute(left, "space", behind)
        if which < len(sets):
            swap_in, other_in = after(arrived, slab)
            terms |= zip(sets[which], factors(which, [swap_in, first[1], other_in]))
        factors_here = [terms[step] for step in rounds[which]]
        begun = pallas(
            functools.partial(interior_kernel, rounds[which], reach),
            "interior",
            [block(FIELDS, 2 * tile)] * 4,
            [VMEM] * (3 + len(factors_here)),
            [scratch(FIELDS, planes)] * 4,
            grant=8,
        )(waves, *factors_here, force, slab)
        outs = advance(which, [*factors_here, force, left_in, right_in, *begun])
    keep, give = outs
    given = lax.ppermute(give, "space", swap)
    mine = parity()
    low, high = jnp.where(mine == 0, keep, given), jnp.where(mine == 0, given, keep)
    return jnp.stack([low, high])


def solution(mesh):
    return jax.shard_map(
        per_device,
        mesh=mesh,
        in_specs=(
            P(("groups", "vec"), None, "space", None, None),
            P(("groups", "vec"), None, "space", None, None),
            P(("groups", "vec")),
            P("vec", None, "space", None, None),
            P(),
        ),
        out_specs=P(("groups", "vec"), None, "space", None, None),
        check_vma=False,
    )
```

```python
import functools

import jax
import jax.numpy as jnp
from jax import lax
from jax.experimental import pallas as pl
from jax.experimental.pallas import tpu as pltpu
from jax.sharding import PartitionSpec as P

HEAT_RATIO = 1.4
VISCOSITY = 0.1
TIME_STEP = 0.4
FIELDS = 5
TERMS = 26
STAGES = 4


VMEM = pl.BlockSpec(memory_space=pltpu.VMEM)
SMEM = pl.BlockSpec(memory_space=pltpu.SMEM)
HBM = pl.BlockSpec(memory_space=pltpu.HBM)


def parity():
    return lax.rem(lax.axis_index("space"), 2)


def in_place(*arrays):
    return [pltpu.with_memory_space_constraint(array, pltpu.HBM) for array in arrays]


def after(values, *earlier):
    return lax.optimization_barrier((values, *earlier))[0]


def pallas(kernel, name, outs, in_specs, scratch=(), grant=4):
    return pl.pallas_call(
        kernel,
        out_shape=outs,
        in_specs=in_specs,
        out_specs=[VMEM] * len(outs),
        scratch_shapes=scratch,
        compiler_params=pltpu.CompilerParams(vmem_limit_bytes=grant << 20),
        name=name,
    )


def pack_kernel(sets, widths, reach, which, phase_slot, pert, force, base, base_peer, *refs):
    count = sum(3 if chosen == 0 else 2 for chosen in which)
    sends, kept, sem = refs[:count], refs[count:-1], refs[-1]
    mine = parity()
    core = lax.axis_index("vec")
    other = 1 - mine
    tile = pert.shape[2]
    local = base.shape[0]
    waits = []

    def copy(source, target, at, count):
        into = target.at[:, pl.ds(at, count)]
        waits.append(pltpu.make_async_copy(source(), into, sem.at[len(waits)]))
        waits[-1].start()

    def copy_base(step, cells, target, at, count):
        into = target.at[:, pl.ds(at, count)]
        held = lax.div(phase_slot[step], local) == core
        row = lax.rem(phase_slot[step], local)
        first, second = [
            pltpu.make_async_copy(array.at[row, :, cells], into, sem.at[len(waits)]) for array in (base, base_peer)
        ]
        pl.when(held)(first.start)
        pl.when(jnp.logical_not(held))(second.start)
        waits.append(first)

    for chosen in which:
        if chosen == 0:
            swap_out, own_out, other_out, *sends = sends
        else:
            swap_out, other_out, *sends = sends
        at_swap = at_other = at_own = 0
        if chosen == 0:
            for array, width in ((pert, widths[0]), (force, reach - 1)):
                edge = pl.ds(mine * (tile - width), width)
                copy(lambda: array.at[other], swap_out, at_swap, tile)
                copy(lambda: array.at[mine, :, edge], own_out, at_own, width)
                copy(lambda: array.at[other, :, edge], other_out, at_other, width)
                at_swap += tile
                at_own += width
                at_other += width
        half = tile // 2
        layers = lambda step: pl.ds(mine * (tile - widths[step]) + core * (widths[step] // 2), widths[step] // 2)
        for step in sets[chosen]:
            copy_base(step, pl.ds(core * half, half), swap_out, at_swap, half)
            copy_base(step, layers(step), other_out, at_other, widths[step] // 2)
            at_swap += half
            at_other += widths[step] // 2
        if chosen == 0:
            for step in sum(sets, []):
                copy_base(step, layers(step), own_out, at_own, widths[step] // 2)
                at_own += widths[step] // 2
    if kept:
        held_state, held_base = kept
        copy(lambda: pert.at[mine], held_state, 0, tile)
        copy(lambda: force.at[mine], held_state, tile, tile)
        for step in range(held_base.shape[1] // tile):
            copy_base(step, pl.ds(0, tile), held_base, step * tile, tile)
    for wait in waits:
        wait.wait()


def waves_kernel(moments, frequency, waves):
    shape = waves.shape[1:]
    rows = lax.broadcasted_iota(jnp.int32, shape, 0)
    for first in range(0, len(moments), shape[0]):
        chunk = moments[first : first + shape[0]]
        angle = jnp.zeros(shape, jnp.float32)
        for row, moment in enumerate(chunk):
            angle = jnp.where(rows == row, moment, angle)
        wave = jnp.cos(frequency[parity()] * angle)
        for row in range(len(chunk)):
            waves[first + row] = jnp.broadcast_to(wave[row : row + 1], shape)


def neighbours(ref, field, at, count):
    block = ref[field, pl.ds(at - 1, count + 2)]
    centre = block[1 : count + 1]
    return (
        centre,
        (block[2:], block[:count]),
        (pltpu.roll(centre, centre.shape[1] - 1, 1), pltpu.roll(centre, 1, 1)),
        (pltpu.roll(centre, centre.shape[2] - 1, 2), pltpu.roll(centre, 1, 2)),
    )


def base_terms(base, terms, at, count):
    centre, diff = [], []
    for field in range(FIELDS):
        mid, along_x, along_y, along_z = neighbours(base, field, at, count)
        centre.append(mid)
        diff.append([up - down for up, down in (along_x, along_y, along_z)])
    density, pressure = centre[0], centre[4]
    inverse = 1.0 / density
    square = 0.5 * inverse * inverse
    divergence = diff[1][0] + diff[2][1] + diff[3][2]
    out = [-0.5 * centre[1 + j] for j in range(3)]
    out += [-0.5 * diff[0][j] for j in range(3)]
    out += [-0.5 * density, -0.5 * divergence]
    for j in range(3):
        for k in range(3):
            slope = -0.5 * diff[1 + k][j]
            out.append(slope - 6.0 * VISCOSITY if j == k else slope)
    out += [-0.5 * inverse]
    out += [diff[4][k] * square for k in range(3)]
    out += [-0.5 * diff[4][j] for j in range(3)]
    out += [-0.5 * HEAT_RATIO * pressure, -0.5 * HEAT_RATIO * divergence]
    for index, value in enumerate(out):
        terms[index, pl.ds(at, count)] = value


def terms_kernel(steps, widths, at_held, starts, reach, held_base, *refs):
    mine_in, peer_in, outs, held = refs[:3], refs[3:6], refs[6:-1], refs[-1]
    mine = parity()
    core = lax.axis_index("vec")
    planes = held.shape[1]
    tile = planes // 2 - reach
    half = tile // 2
    starts = [list(start) for start in starts]
    for step, terms in zip(steps, outs):
        width = widths[step]
        held[:, pl.ds(reach + mine * tile, tile)] = held_base[:, at_held : at_held + tile]
        partner = reach + (1 - mine) * tile
        near, far = reach - width, reach + 2 * tile
        own_at = near + (1 - mine) * (far - near)
        other_at = near + mine * (far - near)
        for (swap_in, own_in, other_in), who, start in zip((mine_in, peer_in), (core, 1 - core), starts):
            edge = width // 2
            at_swap, at_own, at_other = start
            held[:, pl.ds(partner + who * half, half)] = swap_in[:, at_swap : at_swap + half]
            held[:, pl.ds(own_at + who * edge, edge)] = own_in[:, at_own : at_own + edge]
            held[:, pl.ds(other_at + who * edge, edge)] = other_in[:, at_other : at_other + edge]
            start[:] = [at_swap + half, at_own + edge, at_other + edge]
        for at, count in singly([(near + 1, planes - 2 * near - 2)]):
            base_terms(held, terms, at, count)
        at_held += tile


def rates(state, terms, force, wave, at, count):
    here = pl.ds(at, count)
    centre, diff, around = [], [], []
    for field in range(FIELDS):
        mid, along_x, along_y, along_z = neighbours(state, field, at, count)
        centre.append(mid)
        diff.append([up - down for up, down in (along_x, along_y, along_z)])
        if 1 <= field <= 3:
            around.append((along_x[0] + along_x[1]) + (along_y[0] + along_y[1]) + (along_z[0] + along_z[1]))
    term = lambda index: terms[index, here]
    speed = [term(j) for j in range(3)]
    spread = diff[1][0] + diff[2][1] + diff[3][2]

    def carried(field, first, stride):
        total = force[field, here] * wave
        for j in range(3):
            total = total + (speed[j] * diff[field][j] + centre[1 + j] * term(first + stride * j))
        return total

    out = [carried(0, 3, 1) + (term(6) * spread + centre[0] * term(7))]
    inverse = term(17)
    for k in range(3):
        pull = inverse * diff[4][k] + centre[0] * term(18 + k)
        out.append(carried(1 + k, 8 + k, 3) + (pull + VISCOSITY * around[k]))
    out.append(carried(4, 21, 1) + (term(24) * spread + centre[4] * term(25)))
    return out


def singly(ranges):
    return [(at, 1) for first, count in ranges for at in range(first, first + count)]


def one_step(cover, depth, state, force, terms, waves, second, third, fourth):
    def stage(number, source, size, wave, target):
        for at, count in singly(cover(depth + number)):
            here = pl.ds(at, count)
            for field, rate in enumerate(rates(source, terms, force, wave[None], at, count)):
                target[field, here] = state[field, here] + size * rate

    stage(1, state, 0.5 * TIME_STEP, waves[0], second)
    stage(2, second, 0.5 * TIME_STEP, waves[1], third)
    stage(3, third, TIME_STEP, waves[1], fourth)
    for at, count in singly(cover(depth + STAGES)):
        here = pl.ds(at, count)
        for field, rate in enumerate(rates(fourth, terms, force, waves[2][None], at, count)):
            mixed = second[field, here] + fourth[field, here] + 2.0 * third[field, here] - state[field, here]
            state[field, here] = mixed * (1.0 / 3.0) + (TIME_STEP / 6.0) * rate


def several(steps, cover, waves, state, force, terms, *stages):
    for index, step in enumerate(steps):
        wave = [waves[3 * step + which] for which in range(3)]
        one_step(cover, STAGES * index, state, force, terms[index], wave, *stages)


def inner(reach, slab, depth):
    return [(reach + depth, slab - 2 * depth)] if slab > 2 * depth else []


def outer(reach, slab, width, depth):
    low, high = reach - width + depth, reach + slab + width - depth
    if not inner(reach, slab, depth):
        return [(low, high - low)]
    return [(low, width), (high - width, width)]


def interior_kernel(steps, reach, waves, *refs):
    terms, (force, slab, *refs) = refs[: len(steps)], refs[len(steps) :]
    outs, scratch = refs[:4], refs[4:]
    planes = slab.shape[1]
    scratch[0][:, reach : reach + planes] = slab[...]
    several(steps, functools.partial(inner, reach, planes), waves, scratch[0], force, terms, *scratch[1:])
    for index, (out, held) in enumerate(zip(outs, scratch)):
        out[:, index : planes - index] = held[:, reach + index : reach + planes - index]


def advance_kernel(steps, widths, reach, first, last, next_width, waves, *refs):
    terms, refs = refs[: len(steps)], refs[len(steps) :]
    width = widths[steps[0]]
    state, second, third, fourth = refs[-4:]
    refs = refs[:-4]
    planes = state.shape[1]
    tile = planes // 2 - reach
    mine = parity()
    near, far = reach - width, reach + 2 * tile
    if first:
        held_state, swap_in, own_in, other_in, force, *outs = refs
        here, there = pl.ds(reach + mine * tile, tile), pl.ds(reach + (1 - mine) * tile, tile)
        state[:, here] = held_state[:, 0:tile]
        state[:, there] = swap_in[:, 0:tile]
        state[:, pl.ds(near + (1 - mine) * (far - near), width)] = own_in[:, 0:width]
        state[:, pl.ds(near + mine * (far - near), width)] = other_in[:, 0:width]
        force[:, here] = held_state[:, tile : 2 * tile]
        force[:, there] = swap_in[:, tile : 2 * tile]
        layers = reach - 1
        force[:, pl.ds(1 + (1 - mine) * (far - 1), layers)] = own_in[:, width : width + layers]
        force[:, pl.ds(1 + mine * (far - 1), layers)] = other_in[:, width : width + layers]
        cover = lambda depth: [(near + depth, planes - 2 * (near + depth))]
    else:
        force, left_in, right_in, *refs = refs
        begun, outs = refs[:4], refs[4:]
        for index, (source, held) in enumerate(zip(begun, (state, second, third, fourth))):
            held[:, reach + index : far - index] = source[:, index : 2 * tile - index]
        state[:, near:reach] = left_in[...]
        state[:, far : far + width] = right_in[...]
        cover = functools.partial(outer, reach, 2 * tile, width)
    several(steps, cover, waves, state, force, terms, second, third, fourth)
    if last:
        keep, give = outs
        keep[...] = state[:, pl.ds(reach + mine * tile, tile)]
        give[...] = state[:, pl.ds(reach + (1 - mine) * tile, tile)]
    else:
        slab, left, right = outs
        slab[...] = state[:, reach:far]
        left[...] = state[:, reach : reach + next_width]
        right[...] = state[:, far - next_width : far]


def per_device(perturbation, forcing, frequency, base_flow, phase_slot):
    _, _, tile, rows, lanes = perturbation.shape
    count = lax.axis_size("space")
    steps = phase_slot.shape[0]
    block = lambda *lead: jax.ShapeDtypeStruct((*lead, rows, lanes), jnp.float32)
    scratch = lambda *lead: pltpu.VMEM((*lead, rows, lanes), jnp.float32)

    rounds = [list(range(start, min(start + 2, steps))) for start in range(0, steps, 2)]
    sets = [each for each in (rounds[0], sum(rounds[1:], [])) if each]
    widths = {step: STAGES * (each[-1] - step + 1) for each in rounds for step in each}
    reach = max(widths.values())
    state_edge = widths[0] + reach - 1
    planes = 2 * (tile + reach)

    swap = [(i, i ^ 1) for i in range(count)]
    own = [(i, (i + 2 * (1 if i % 2 else -1)) % count) for i in range(count)]
    other = [(i, (i + (1 if i % 2 else -1)) % count) for i in range(count)]
    ahead = [(i, (i + 2) % count) for i in range(count)]
    behind = [(i, (i - 2) % count) for i in range(count)]
    core = [(0, 1), (1, 0)]

    base_peer = lax.ppermute(base_flow, "vec", core)
    moments = [step * TIME_STEP + part for step in range(steps) for part in (0.0, 0.5 * TIME_STEP, TIME_STEP)]

    def pack(which, keep):
        sends, copies = [], 0
        for chosen in which:
            group, start = sets[chosen], chosen == 0
            swapped = len(group) * (tile // 2) + (2 * tile if start else 0)
            edges = sum(widths[step] // 2 for step in group) + (state_edge if start else 0)
            every = sum(widths.values()) // 2 + state_edge
            sends += [block(FIELDS, swapped)] + ([block(FIELDS, every)] if start else []) + [block(FIELDS, edges)]
            copies += 2 * len(group) + (6 + steps if start else 0)
        kept = [block(FIELDS, 2 * tile), block(FIELDS, steps * tile)] if keep else []
        return pallas(
            functools.partial(pack_kernel, sets, widths, reach, which),
            "pack",
            sends + kept,
            [SMEM] + [HBM] * 4,
            [pltpu.SemaphoreType.DMA((copies + (2 + steps if keep else 0),))],
        )(*in_place(phase_slot, perturbation, forcing, base_flow), base_peer)

    def exchange(packed, perms):
        return [lax.ppermute(part, "space", perm) for part, perm in zip(packed, perms)]

    def factors(which, arrived):
        group = sets[which]
        edges = sum(widths[step] // 2 for step in group)
        starts = [2 * tile, state_edge, state_edge] if which == 0 else [0, 0, 0]
        if which > 0:
            starts[1] = state_edge + sum(widths[step] // 2 for each in sets[:which] for step in each)
        sizes = (len(group) * tile // 2, edges, edges)
        parts = [part[:, at : at + size] for part, at, size in zip(arrived, starts, sizes)]
        if which == 0:
            crossed, others = [lax.ppermute(part, "vec", core) for part in parts], (0, 0, 0)
        else:
            crossed = [lax.ppermute(jnp.concatenate(parts, axis=1), "vec", core)] * 3
            others = (0, sizes[0], sizes[0] + edges)
        return pallas(
            functools.partial(terms_kernel, group, widths, group[0] * tile, (starts, others), reach),
            "terms",
            [block(TERMS, planes)] * len(group),
            [VMEM] * 7,
            [scratch(FIELDS, planes)],
            grant=2,
        )(held_base, *arrived, *crossed)

    def advance(which, operands):
        group = rounds[which]
        first, last = which == 0, which == len(rounds) - 1
        next_width = 0 if last else widths[rounds[which + 1][0]]
        if last:
            outs = [block(FIELDS, tile)] * 2
        else:
            outs = [block(FIELDS, 2 * tile), block(FIELDS, next_width), block(FIELDS, next_width)]
        if first:
            outs = [block(FIELDS, planes)] + outs
        return pallas(
            functools.partial(advance_kernel, group, widths, reach, first, last, next_width),
            "advance",
            outs,
            [VMEM] * (1 + len(operands)),
            [scratch(FIELDS, planes)] * 4,
            grant=8,
        )(waves, *operands)

    first = exchange(pack([0], False), (swap, own, other))
    *later, held_state, held_base = pack(range(1, len(sets)), True)
    (waves,) = pallas(functools.partial(waves_kernel, moments), "waves", [block(3 * steps)], [SMEM])(*in_place(frequency))
    arrived = exchange(later, (swap, other))
    first, held_state, held_base, waves = lax.optimization_barrier((first, held_state, held_base, waves))
    terms = dict(zip(sets[0], factors(0, first)))
    force, *outs = advance(0, [*[terms[step] for step in rounds[0]], held_state, *first])
    for which in range(1, len(rounds)):
        slab, left, right = outs
        left_in = lax.ppermute(right, "space", ahead)
        right_in = lax.ppermute(left, "space", behind)
        if which < len(sets):
            swap_in, other_in = after(arrived, slab)
            terms |= zip(sets[which], factors(which, [swap_in, first[1], other_in]))
        factors_here = [terms[step] for step in rounds[which]]
        begun = pallas(
            functools.partial(interior_kernel, rounds[which], reach),
            "interior",
            [block(FIELDS, 2 * tile)] * 4,
            [VMEM] * (3 + len(factors_here)),
            [scratch(FIELDS, planes)] * 4,
            grant=8,
        )(waves, *factors_here, force, slab)
        outs = advance(which, [*factors_here, force, left_in, right_in, *begun])
    keep, give = outs
    given = lax.ppermute(give, "space", swap)
    mine = parity()
    low, high = jnp.where(mine == 0, keep, given), jnp.where(mine == 0, given, keep)
    return jnp.stack([low, high])


def solution(mesh):
    return jax.shard_map(
        per_device,
        mesh=mesh,
        in_specs=(
            P(("groups", "vec"), None, "space", None, None),
            P(("groups", "vec"), None, "space", None, None),
            P(("groups", "vec")),
            P("vec", None, "space", None, None),
            P(),
        ),
        out_specs=P(("groups", "vec"), None, "space", None, None),
        check_vma=False,
    )
```

```python
import functools

import jax
import jax.numpy as jnp
from jax import lax
from jax.experimental import pallas as pl
from jax.experimental.pallas import tpu as pltpu
from jax.sharding import PartitionSpec as P

HEAT_RATIO = 1.4
VISCOSITY = 0.1
TIME_STEP = 0.4
FIELDS = 5
TERMS = 26
STAGES = 4


VMEM = pl.BlockSpec(memory_space=pltpu.VMEM)
SMEM = pl.BlockSpec(memory_space=pltpu.SMEM)
HBM = pl.BlockSpec(memory_space=pltpu.HBM)


def parity():
    return lax.rem(lax.axis_index("space"), 2)


def in_place(*arrays):
    return [pltpu.with_memory_space_constraint(array, pltpu.HBM) for array in arrays]


def after(values, *earlier):
    return lax.optimization_barrier((values, *earlier))[0]


def pallas(kernel, name, outs, in_specs, scratch=(), grant=4):
    return pl.pallas_call(
        kernel,
        out_shape=outs,
        in_specs=in_specs,
        out_specs=[VMEM] * len(outs),
        scratch_shapes=scratch,
        compiler_params=pltpu.CompilerParams(vmem_limit_bytes=grant << 20),
        name=name,
    )


def pack_kernel(sets, widths, reach, which, phase_slot, pert, force, base, base_peer, *refs):
    count = sum(3 if chosen == 0 else 2 for chosen in which)
    sends, kept, (slots, sem) = refs[:count], refs[count:-2], refs[-2:]
    fetched = pltpu.make_async_copy(phase_slot, slots, sem.at[sem.shape[0] - 1])
    fetched.start()
    waiting = [fetched]
    mine = parity()
    core = lax.axis_index("vec")
    other = 1 - mine
    tile = pert.shape[2]
    local = base.shape[0]
    waits = []

    def copy(source, target, at, count):
        into = target.at[:, pl.ds(at, count)]
        waits.append(pltpu.make_async_copy(source(), into, sem.at[len(waits)]))
        waits[-1].start()

    def copy_base(step, cells, target, at, count):
        if waiting:
            waiting.pop().wait()
        into = target.at[:, pl.ds(at, count)]
        held = lax.div(slots[step], local) == core
        row = lax.rem(slots[step], local)
        first, second = [
            pltpu.make_async_copy(array.at[row, :, cells], into, sem.at[len(waits)]) for array in (base, base_peer)
        ]
        pl.when(held)(first.start)
        pl.when(jnp.logical_not(held))(second.start)
        waits.append(first)

    for chosen in which:
        if chosen == 0:
            swap_out, own_out, other_out, *sends = sends
        else:
            swap_out, other_out, *sends = sends
        at_swap = at_other = at_own = 0
        if chosen == 0:
            for array, width in ((pert, widths[0]), (force, reach - 1)):
                edge = pl.ds(mine * (tile - width), width)
                copy(lambda: array.at[other], swap_out, at_swap, tile)
                copy(lambda: array.at[mine, :, edge], own_out, at_own, width)
                copy(lambda: array.at[other, :, edge], other_out, at_other, width)
                at_swap += tile
                at_own += width
                at_other += width
        half = tile // 2
        layers = lambda step: pl.ds(mine * (tile - widths[step]) + core * (widths[step] // 2), widths[step] // 2)
        for step in sets[chosen]:
            copy_base(step, pl.ds(core * half, half), swap_out, at_swap, half)
            copy_base(step, layers(step), other_out, at_other, widths[step] // 2)
            at_swap += half
            at_other += widths[step] // 2
        if chosen == 0:
            for step in sum(sets, []):
                copy_base(step, layers(step), own_out, at_own, widths[step] // 2)
                at_own += widths[step] // 2
    if kept:
        held_state, held_base = kept
        copy(lambda: pert.at[mine], held_state, 0, tile)
        copy(lambda: force.at[mine], held_state, tile, tile)
        for step in range(held_base.shape[1] // tile):
            copy_base(step, pl.ds(0, tile), held_base, step * tile, tile)
    for wait in waits:
        wait.wait()


def waves_kernel(moments, frequency, waves):
    shape = waves.shape[1:]
    rows = lax.broadcasted_iota(jnp.int32, shape, 0)
    for first in range(0, len(moments), shape[0]):
        chunk = moments[first : first + shape[0]]
        angle = jnp.zeros(shape, jnp.float32)
        for row, moment in enumerate(chunk):
            angle = jnp.where(rows == row, moment, angle)
        wave = jnp.cos(frequency[parity()] * angle)
        for row in range(len(chunk)):
            waves[first + row] = jnp.broadcast_to(wave[row : row + 1], shape)


def neighbours(ref, field, at, count):
    block = ref[field, pl.ds(at - 1, count + 2)]
    centre = block[1 : count + 1]
    return (
        centre,
        (block[2:], block[:count]),
        (pltpu.roll(centre, centre.shape[1] - 1, 1), pltpu.roll(centre, 1, 1)),
        (pltpu.roll(centre, centre.shape[2] - 1, 2), pltpu.roll(centre, 1, 2)),
    )


def base_terms(base, terms, at, count):
    centre, diff = [], []
    for field in range(FIELDS):
        mid, along_x, along_y, along_z = neighbours(base, field, at, count)
        centre.append(mid)
        diff.append([up - down for up, down in (along_x, along_y, along_z)])
    density, pressure = centre[0], centre[4]
    inverse = 1.0 / density
    square = 0.5 * inverse * inverse
    divergence = diff[1][0] + diff[2][1] + diff[3][2]
    out = [-0.5 * centre[1 + j] for j in range(3)]
    out += [-0.5 * diff[0][j] for j in range(3)]
    out += [-0.5 * density, -0.5 * divergence]
    for j in range(3):
        for k in range(3):
            slope = -0.5 * diff[1 + k][j]
            out.append(slope - 6.0 * VISCOSITY if j == k else slope)
    out += [-0.5 * inverse]
    out += [diff[4][k] * square for k in range(3)]
    out += [-0.5 * diff[4][j] for j in range(3)]
    out += [-0.5 * HEAT_RATIO * pressure, -0.5 * HEAT_RATIO * divergence]
    for index, value in enumerate(out):
        terms[index, pl.ds(at, count)] = value


def terms_kernel(steps, widths, at_held, starts, reach, held_base, *refs):
    mine_in, peer_in, outs, held = refs[:3], refs[3:6], refs[6:-1], refs[-1]
    mine = parity()
    core = lax.axis_index("vec")
    planes = held.shape[1]
    tile = planes // 2 - reach
    half = tile // 2
    starts = [list(start) for start in starts]
    for step, terms in zip(steps, outs):
        width = widths[step]
        held[:, pl.ds(reach + mine * tile, tile)] = held_base[:, at_held : at_held + tile]
        partner = reach + (1 - mine) * tile
        near, far = reach - width, reach + 2 * tile
        own_at = near + (1 - mine) * (far - near)
        other_at = near + mine * (far - near)
        for (swap_in, own_in, other_in), who, start in zip((mine_in, peer_in), (core, 1 - core), starts):
            edge = width // 2
            at_swap, at_own, at_other = start
            held[:, pl.ds(partner + who * half, half)] = swap_in[:, at_swap : at_swap + half]
            held[:, pl.ds(own_at + who * edge, edge)] = own_in[:, at_own : at_own + edge]
            held[:, pl.ds(other_at + who * edge, edge)] = other_in[:, at_other : at_other + edge]
            start[:] = [at_swap + half, at_own + edge, at_other + edge]
        for at, count in singly([(near + 1, planes - 2 * near - 2)]):
            base_terms(held, terms, at, count)
        at_held += tile


def rates(state, terms, force, wave, at, count):
    here = pl.ds(at, count)
    centre, diff, around = [], [], []
    for field in range(FIELDS):
        mid, along_x, along_y, along_z = neighbours(state, field, at, count)
        centre.append(mid)
        diff.append([up - down for up, down in (along_x, along_y, along_z)])
        if 1 <= field <= 3:
            around.append((along_x[0] + along_x[1]) + (along_y[0] + along_y[1]) + (along_z[0] + along_z[1]))
    term = lambda index: terms[index, here]
    speed = [term(j) for j in range(3)]
    spread = diff[1][0] + diff[2][1] + diff[3][2]

    def carried(field, first, stride):
        total = force[field, here] * wave
        for j in range(3):
            total = total + (speed[j] * diff[field][j] + centre[1 + j] * term(first + stride * j))
        return total

    out = [carried(0, 3, 1) + (term(6) * spread + centre[0] * term(7))]
    inverse = term(17)
    for k in range(3):
        pull = inverse * diff[4][k] + centre[0] * term(18 + k)
        out.append(carried(1 + k, 8 + k, 3) + (pull + VISCOSITY * around[k]))
    out.append(carried(4, 21, 1) + (term(24) * spread + centre[4] * term(25)))
    return out


def singly(ranges):
    return [(at, 1) for first, count in ranges for at in range(first, first + count)]


def one_step(cover, depth, state, force, terms, waves, second, third, fourth):
    def stage(number, source, size, wave, target):
        for at, count in singly(cover(depth + number)):
            here = pl.ds(at, count)
            for field, rate in enumerate(rates(source, terms, force, wave[None], at, count)):
                target[field, here] = state[field, here] + size * rate

    stage(1, state, 0.5 * TIME_STEP, waves[0], second)
    stage(2, second, 0.5 * TIME_STEP, waves[1], third)
    stage(3, third, TIME_STEP, waves[1], fourth)
    for at, count in singly(cover(depth + STAGES)):
        here = pl.ds(at, count)
        for field, rate in enumerate(rates(fourth, terms, force, waves[2][None], at, count)):
            mixed = second[field, here] + fourth[field, here] + 2.0 * third[field, here] - state[field, here]
            state[field, here] = mixed * (1.0 / 3.0) + (TIME_STEP / 6.0) * rate


def several(steps, cover, waves, state, force, terms, *stages):
    for index, step in enumerate(steps):
        wave = [waves[3 * step + which] for which in range(3)]
        one_step(cover, STAGES * index, state, force, terms[index], wave, *stages)


def inner(reach, slab, depth):
    return [(reach + depth, slab - 2 * depth)] if slab > 2 * depth else []


def outer(reach, slab, width, depth):
    low, high = reach - width + depth, reach + slab + width - depth
    if not inner(reach, slab, depth):
        return [(low, high - low)]
    return [(low, width), (high - width, width)]


def interior_kernel(steps, reach, waves, *refs):
    terms, (force, slab, *refs) = refs[: len(steps)], refs[len(steps) :]
    outs, scratch = refs[:4], refs[4:]
    planes = slab.shape[1]
    scratch[0][:, reach : reach + planes] = slab[...]
    several(steps, functools.partial(inner, reach, planes), waves, scratch[0], force, terms, *scratch[1:])
    for index, (out, held) in enumerate(zip(outs, scratch)):
        out[:, index : planes - index] = held[:, reach + index : reach + planes - index]


def advance_kernel(steps, widths, reach, first, last, next_width, waves, *refs):
    terms, refs = refs[: len(steps)], refs[len(steps) :]
    width = widths[steps[0]]
    state, second, third, fourth = refs[-4:]
    refs = refs[:-4]
    planes = state.shape[1]
    tile = planes // 2 - reach
    mine = parity()
    near, far = reach - width, reach + 2 * tile
    if first:
        held_state, swap_in, own_in, other_in, force, *outs = refs
        here, there = pl.ds(reach + mine * tile, tile), pl.ds(reach + (1 - mine) * tile, tile)
        state[:, here] = held_state[:, 0:tile]
        state[:, there] = swap_in[:, 0:tile]
        state[:, pl.ds(near + (1 - mine) * (far - near), width)] = own_in[:, 0:width]
        state[:, pl.ds(near + mine * (far - near), width)] = other_in[:, 0:width]
        force[:, here] = held_state[:, tile : 2 * tile]
        force[:, there] = swap_in[:, tile : 2 * tile]
        layers = reach - 1
        force[:, pl.ds(1 + (1 - mine) * (far - 1), layers)] = own_in[:, width : width + layers]
        force[:, pl.ds(1 + mine * (far - 1), layers)] = other_in[:, width : width + layers]
        cover = lambda depth: [(near + depth, planes - 2 * (near + depth))]
    else:
        force, left_in, right_in, *refs = refs
        begun, outs = refs[:4], refs[4:]
        for index, (source, held) in enumerate(zip(begun, (state, second, third, fourth))):
            held[:, reach + index : far - index] = source[:, index : 2 * tile - index]
        state[:, near:reach] = left_in[...]
        state[:, far : far + width] = right_in[...]
        cover = functools.partial(outer, reach, 2 * tile, width)
    several(steps, cover, waves, state, force, terms, second, third, fourth)
    if last:
        keep, give = outs
        keep[...] = state[:, pl.ds(reach + mine * tile, tile)]
        give[...] = state[:, pl.ds(reach + (1 - mine) * tile, tile)]
    else:
        slab, left, right = outs
        slab[...] = state[:, reach:far]
        left[...] = state[:, reach : reach + next_width]
        right[...] = state[:, far - next_width : far]


def per_device(perturbation, forcing, frequency, base_flow, phase_slot):
    _, _, tile, rows, lanes = perturbation.shape
    count = lax.axis_size("space")
    steps = phase_slot.shape[0]
    block = lambda *lead: jax.ShapeDtypeStruct((*lead, rows, lanes), jnp.float32)
    scratch = lambda *lead: pltpu.VMEM((*lead, rows, lanes), jnp.float32)

    rounds = [list(range(start, min(start + 2, steps))) for start in range(0, steps, 2)]
    sets = [each for each in (rounds[0], sum(rounds[1:], [])) if each]
    widths = {step: STAGES * (each[-1] - step + 1) for each in rounds for step in each}
    reach = max(widths.values())
    state_edge = widths[0] + reach - 1
    planes = 2 * (tile + reach)

    swap = [(i, i ^ 1) for i in range(count)]
    own = [(i, (i + 2 * (1 if i % 2 else -1)) % count) for i in range(count)]
    other = [(i, (i + (1 if i % 2 else -1)) % count) for i in range(count)]
    ahead = [(i, (i + 2) % count) for i in range(count)]
    behind = [(i, (i - 2) % count) for i in range(count)]
    core = [(0, 1), (1, 0)]

    base_peer = lax.ppermute(base_flow, "vec", core)
    moments = [step * TIME_STEP + part for step in range(steps) for part in (0.0, 0.5 * TIME_STEP, TIME_STEP)]

    def pack(which, keep):
        sends, copies = [], 0
        for chosen in which:
            group, start = sets[chosen], chosen == 0
            swapped = len(group) * (tile // 2) + (2 * tile if start else 0)
            edges = sum(widths[step] // 2 for step in group) + (state_edge if start else 0)
            every = sum(widths.values()) // 2 + state_edge
            sends += [block(FIELDS, swapped)] + ([block(FIELDS, every)] if start else []) + [block(FIELDS, edges)]
            copies += 2 * len(group) + (6 + steps if start else 0)
        kept = [block(FIELDS, 2 * tile), block(FIELDS, steps * tile)] if keep else []
        return pallas(
            functools.partial(pack_kernel, sets, widths, reach, which),
            "pack",
            sends + kept,
            [HBM] * 5,
            [pltpu.SMEM(phase_slot.shape, jnp.int32), pltpu.SemaphoreType.DMA((copies + (3 + steps if keep else 1),))],
        )(*in_place(phase_slot, perturbation, forcing, base_flow), base_peer)

    def exchange(packed, perms):
        return [lax.ppermute(part, "space", perm) for part, perm in zip(packed, perms)]

    def factors(which, arrived):
        group = sets[which]
        edges = sum(widths[step] // 2 for step in group)
        starts = [2 * tile, state_edge, state_edge] if which == 0 else [0, 0, 0]
        if which > 0:
            starts[1] = state_edge + sum(widths[step] // 2 for each in sets[:which] for step in each)
        sizes = (len(group) * tile // 2, edges, edges)
        parts = [part[:, at : at + size] for part, at, size in zip(arrived, starts, sizes)]
        if which == 0:
            crossed, others = [lax.ppermute(part, "vec", core) for part in parts], (0, 0, 0)
        else:
            crossed = [lax.ppermute(jnp.concatenate(parts, axis=1), "vec", core)] * 3
            others = (0, sizes[0], sizes[0] + edges)
        return pallas(
            functools.partial(terms_kernel, group, widths, group[0] * tile, (starts, others), reach),
            "terms",
            [block(TERMS, planes)] * len(group),
            [VMEM] * 7,
            [scratch(FIELDS, planes)],
            grant=2,
        )(held_base, *arrived, *crossed)

    def advance(which, operands):
        group = rounds[which]
        first, last = which == 0, which == len(rounds) - 1
        next_width = 0 if last else widths[rounds[which + 1][0]]
        if last:
            outs = [block(FIELDS, tile)] * 2
        else:
            outs = [block(FIELDS, 2 * tile), block(FIELDS, next_width), block(FIELDS, next_width)]
        if first:
            outs = [block(FIELDS, planes)] + outs
        return pallas(
            functools.partial(advance_kernel, group, widths, reach, first, last, next_width),
            "advance",
            outs,
            [VMEM] * (1 + len(operands)),
            [scratch(FIELDS, planes)] * 4,
            grant=8,
        )(waves, *operands)

    first = exchange(pack([0], False), (swap, own, other))
    *later, held_state, held_base = pack(range(1, len(sets)), True)
    (waves,) = pallas(functools.partial(waves_kernel, moments), "waves", [block(3 * steps)], [SMEM])(*in_place(frequency))
    arrived = exchange(later, (swap, other))
    first, held_state, held_base, waves = lax.optimization_barrier((first, held_state, held_base, waves))
    terms = dict(zip(sets[0], factors(0, first)))
    force, *outs = advance(0, [*[terms[step] for step in rounds[0]], held_state, *first])
    for which in range(1, len(rounds)):
        slab, left, right = outs
        left_in = lax.ppermute(right, "space", ahead)
        right_in = lax.ppermute(left, "space", behind)
        if which < len(sets):
            swap_in, other_in = after(arrived, slab)
            terms |= zip(sets[which], factors(which, [swap_in, first[1], other_in]))
        factors_here = [terms[step] for step in rounds[which]]
        begun = pallas(
            functools.partial(interior_kernel, rounds[which], reach),
            "interior",
            [block(FIELDS, 2 * tile)] * 4,
            [VMEM] * (3 + len(factors_here)),
            [scratch(FIELDS, planes)] * 4,
            grant=8,
        )(waves, *factors_here, force, slab)
        outs = advance(which, [*factors_here, force, left_in, right_in, *begun])
    keep, give = outs
    given = lax.ppermute(give, "space", swap)
    mine = parity()
    low, high = jnp.where(mine == 0, keep, given), jnp.where(mine == 0, given, keep)
    return jnp.stack([low, high])


def solution(mesh):
    return jax.shard_map(
        per_device,
        mesh=mesh,
        in_specs=(
            P(("groups", "vec"), None, "space", None, None),
            P(("groups", "vec"), None, "space", None, None),
            P(("groups", "vec")),
            P("vec", None, "space", None, None),
            P(),
        ),
        out_specs=P(("groups", "vec"), None, "space", None, None),
        check_vma=False,
    )
```

```python
import functools

import jax
import jax.numpy as jnp
from jax import lax
from jax.experimental import pallas as pl
from jax.experimental.pallas import tpu as pltpu
from jax.sharding import PartitionSpec as P

HEAT_RATIO = 1.4
VISCOSITY = 0.1
TIME_STEP = 0.4
FIELDS = 5
TERMS = 26
STAGES = 4


VMEM = pl.BlockSpec(memory_space=pltpu.VMEM)
SMEM = pl.BlockSpec(memory_space=pltpu.SMEM)
HBM = pl.BlockSpec(memory_space=pltpu.HBM)


def parity():
    return lax.rem(lax.axis_index("space"), 2)


def in_place(*arrays):
    return [pltpu.with_memory_space_constraint(array, pltpu.HBM) for array in arrays]


def after(values, *earlier):
    return lax.optimization_barrier((values, *earlier))[0]


def pallas(kernel, name, outs, in_specs, scratch=(), grant=4):
    return pl.pallas_call(
        kernel,
        out_shape=outs,
        in_specs=in_specs,
        out_specs=[VMEM] * len(outs),
        scratch_shapes=scratch,
        compiler_params=pltpu.CompilerParams(vmem_limit_bytes=grant << 20),
        name=name,
    )


def pack_kernel(sets, widths, reach, which, phase_slot, pert, force, base, base_peer, *refs):
    count = sum(3 if chosen == 0 else 2 for chosen in which)
    sends, kept, (slots, sem) = refs[:count], refs[count:-2], refs[-2:]
    fetched = pltpu.make_async_copy(phase_slot, slots, sem.at[sem.shape[0] - 1])
    fetched.start()
    waiting = [fetched]
    mine = parity()
    core = lax.axis_index("vec")
    other = 1 - mine
    tile = pert.shape[2]
    local = base.shape[0]
    waits = []

    def copy(source, target, at, count):
        into = target.at[:, pl.ds(at, count)]
        waits.append(pltpu.make_async_copy(source(), into, sem.at[len(waits)]))
        waits[-1].start()

    def copy_base(step, cells, target, at, count):
        if waiting:
            waiting.pop().wait()
        into = target.at[:, pl.ds(at, count)]
        held = lax.div(slots[step], local) == core
        row = lax.rem(slots[step], local)
        first, second = [
            pltpu.make_async_copy(array.at[row, :, cells], into, sem.at[len(waits)]) for array in (base, base_peer)
        ]
        pl.when(held)(first.start)
        pl.when(jnp.logical_not(held))(second.start)
        waits.append(first)

    for chosen in which:
        if chosen == 0:
            swap_out, own_out, other_out, *sends = sends
        else:
            swap_out, other_out, *sends = sends
        at_swap = at_other = at_own = 0
        if chosen == 0:
            for array, width in ((pert, widths[0]), (force, reach - 1)):
                edge = pl.ds(mine * (tile - width), width)
                copy(lambda: array.at[other], swap_out, at_swap, tile)
                copy(lambda: array.at[mine, :, edge], own_out, at_own, width)
                copy(lambda: array.at[other, :, edge], other_out, at_other, width)
                at_swap += tile
                at_own += width
                at_other += width
        half = tile // 2
        layers = lambda step: pl.ds(mine * (tile - widths[step]) + core * (widths[step] // 2), widths[step] // 2)
        for step in sets[chosen]:
            copy_base(step, pl.ds(core * half, half), swap_out, at_swap, half)
            copy_base(step, layers(step), other_out, at_other, widths[step] // 2)
            at_swap += half
            at_other += widths[step] // 2
        if chosen == 0:
            for step in sum(sets, []):
                copy_base(step, layers(step), own_out, at_own, widths[step] // 2)
                at_own += widths[step] // 2
    if kept:
        held_state, held_base = kept
        copy(lambda: pert.at[mine], held_state, 0, tile)
        copy(lambda: force.at[mine], held_state, tile, tile)
        for step in range(held_base.shape[1] // tile):
            copy_base(step, pl.ds(0, tile), held_base, step * tile, tile)
    for wait in waits:
        wait.wait()


def waves_kernel(moments, frequency, waves):
    shape = waves.shape[1:]
    rows = lax.broadcasted_iota(jnp.int32, shape, 0)
    for first in range(0, len(moments), shape[0]):
        chunk = moments[first : first + shape[0]]
        angle = jnp.zeros(shape, jnp.float32)
        for row, moment in enumerate(chunk):
            angle = jnp.where(rows == row, moment, angle)
        wave = jnp.cos(frequency[parity()] * angle)
        for row in range(len(chunk)):
            waves[first + row] = jnp.broadcast_to(wave[row : row + 1], shape)


def neighbours(ref, field, at, count):
    block = ref[field, pl.ds(at - 1, count + 2)]
    centre = block[1 : count + 1]
    return (
        centre,
        (block[2:], block[:count]),
        (pltpu.roll(centre, centre.shape[1] - 1, 1), pltpu.roll(centre, 1, 1)),
        (pltpu.roll(centre, centre.shape[2] - 1, 2), pltpu.roll(centre, 1, 2)),
    )


def base_terms(base, terms, at, count):
    centre, diff = [], []
    for field in range(FIELDS):
        mid, along_x, along_y, along_z = neighbours(base, field, at, count)
        centre.append(mid)
        diff.append([up - down for up, down in (along_x, along_y, along_z)])
    density, pressure = centre[0], centre[4]
    inverse = 1.0 / density
    square = 0.5 * inverse * inverse
    divergence = diff[1][0] + diff[2][1] + diff[3][2]
    out = [-0.5 * centre[1 + j] for j in range(3)]
    out += [-0.5 * diff[0][j] for j in range(3)]
    out += [-0.5 * density, -0.5 * divergence]
    for j in range(3):
        for k in range(3):
            slope = -0.5 * diff[1 + k][j]
            out.append(slope - 6.0 * VISCOSITY if j == k else slope)
    out += [-0.5 * inverse]
    out += [diff[4][k] * square for k in range(3)]
    out += [-0.5 * diff[4][j] for j in range(3)]
    out += [-0.5 * HEAT_RATIO * pressure, -0.5 * HEAT_RATIO * divergence]
    for index, value in enumerate(out):
        terms[index, pl.ds(at, count)] = value


def terms_kernel(steps, widths, at_held, starts, reach, held_base, *refs):
    mine_in, peer_in, outs, held = refs[:3], refs[3:6], refs[6:-1], refs[-1]
    mine = parity()
    core = lax.axis_index("vec")
    planes = held.shape[1]
    tile = planes // 2 - reach
    half = tile // 2
    starts = [list(start) for start in starts]
    for step, terms in zip(steps, outs):
        width = widths[step]
        held[:, pl.ds(reach + mine * tile, tile)] = held_base[:, at_held : at_held + tile]
        partner = reach + (1 - mine) * tile
        near, far = reach - width, reach + 2 * tile
        own_at = near + (1 - mine) * (far - near)
        other_at = near + mine * (far - near)
        for (swap_in, own_in, other_in), who, start in zip((mine_in, peer_in), (core, 1 - core), starts):
            edge = width // 2
            at_swap, at_own, at_other = start
            held[:, pl.ds(partner + who * half, half)] = swap_in[:, at_swap : at_swap + half]
            held[:, pl.ds(own_at + who * edge, edge)] = own_in[:, at_own : at_own + edge]
            held[:, pl.ds(other_at + who * edge, edge)] = other_in[:, at_other : at_other + edge]
            start[:] = [at_swap + half, at_own + edge, at_other + edge]
        for at, count in singly([(near + 1, planes - 2 * near - 2)]):
            base_terms(held, terms, at, count)
        at_held += tile


def rates(state, terms, force, wave, at, count):
    here = pl.ds(at, count)
    centre, diff, around = [], [], []
    for field in range(FIELDS):
        mid, along_x, along_y, along_z = neighbours(state, field, at, count)
        centre.append(mid)
        diff.append([up - down for up, down in (along_x, along_y, along_z)])
        if 1 <= field <= 3:
            around.append((along_x[0] + along_x[1]) + (along_y[0] + along_y[1]) + (along_z[0] + along_z[1]))
    term = lambda index: terms[index, here]
    speed = [term(j) for j in range(3)]
    spread = diff[1][0] + diff[2][1] + diff[3][2]

    def carried(field, first, stride):
        total = force[field, here] * wave
        for j in range(3):
            total = total + (speed[j] * diff[field][j] + centre[1 + j] * term(first + stride * j))
        return total

    out = [carried(0, 3, 1) + (term(6) * spread + centre[0] * term(7))]
    inverse = term(17)
    for k in range(3):
        pull = inverse * diff[4][k] + centre[0] * term(18 + k)
        out.append(carried(1 + k, 8 + k, 3) + (pull + VISCOSITY * around[k]))
    out.append(carried(4, 21, 1) + (term(24) * spread + centre[4] * term(25)))
    return out


def singly(ranges):
    return [(at, 1) for first, count in ranges for at in range(first, first + count)]


def one_step(cover, depth, state, force, terms, waves, second, third, fourth):
    def stage(number, source, size, wave, target):
        for at, count in singly(cover(depth + number)):
            here = pl.ds(at, count)
            for field, rate in enumerate(rates(source, terms, force, wave[None], at, count)):
                target[field, here] = state[field, here] + size * rate

    stage(1, state, 0.5 * TIME_STEP, waves[0], second)
    stage(2, second, 0.5 * TIME_STEP, waves[1], third)
    stage(3, third, TIME_STEP, waves[1], fourth)
    for at, count in singly(cover(depth + STAGES)):
        here = pl.ds(at, count)
        for field, rate in enumerate(rates(fourth, terms, force, waves[2][None], at, count)):
            mixed = second[field, here] + fourth[field, here] + 2.0 * third[field, here] - state[field, here]
            state[field, here] = mixed * (1.0 / 3.0) + (TIME_STEP / 6.0) * rate


def several(steps, cover, waves, state, force, terms, *stages):
    for index, step in enumerate(steps):
        wave = [waves[3 * step + which] for which in range(3)]
        one_step(cover, STAGES * index, state, force, terms[index], wave, *stages)


def inner(reach, slab, depth):
    return [(reach + depth, slab - 2 * depth)] if slab > 2 * depth else []


def outer(reach, slab, width, depth):
    low, high = reach - width + depth, reach + slab + width - depth
    if not inner(reach, slab, depth):
        return [(low, high - low)]
    return [(low, width), (high - width, width)]


def interior_kernel(steps, reach, waves, *refs):
    terms, (force, slab, *refs) = refs[: len(steps)], refs[len(steps) :]
    outs, scratch = refs[:4], refs[4:]
    planes = slab.shape[1]
    scratch[0][:, reach : reach + planes] = slab[...]
    several(steps, functools.partial(inner, reach, planes), waves, scratch[0], force, terms, *scratch[1:])
    for index, (out, held) in enumerate(zip(outs, scratch)):
        out[:, index : planes - index] = held[:, reach + index : reach + planes - index]


def advance_kernel(steps, widths, reach, first, last, next_width, waves, *refs):
    terms, refs = refs[: len(steps)], refs[len(steps) :]
    width = widths[steps[0]]
    state, second, third, fourth = refs[-4:]
    refs = refs[:-4]
    planes = state.shape[1]
    tile = planes // 2 - reach
    mine = parity()
    near, far = reach - width, reach + 2 * tile
    if first:
        held_state, swap_in, own_in, other_in, force, *outs = refs
        here, there = pl.ds(reach + mine * tile, tile), pl.ds(reach + (1 - mine) * tile, tile)
        state[:, here] = held_state[:, 0:tile]
        state[:, there] = swap_in[:, 0:tile]
        state[:, pl.ds(near + (1 - mine) * (far - near), width)] = own_in[:, 0:width]
        state[:, pl.ds(near + mine * (far - near), width)] = other_in[:, 0:width]
        force[:, here] = held_state[:, tile : 2 * tile]
        force[:, there] = swap_in[:, tile : 2 * tile]
        layers = reach - 1
        force[:, pl.ds(1 + (1 - mine) * (far - 1), layers)] = own_in[:, width : width + layers]
        force[:, pl.ds(1 + mine * (far - 1), layers)] = other_in[:, width : width + layers]
        cover = lambda depth: [(near + depth, planes - 2 * (near + depth))]
    else:
        force, left_in, right_in, *refs = refs
        begun, outs = refs[:4], refs[4:]
        for index, (source, held) in enumerate(zip(begun, (state, second, third, fourth))):
            held[:, reach + index : far - index] = source[:, index : 2 * tile - index]
        state[:, near:reach] = left_in[...]
        state[:, far : far + width] = right_in[...]
        cover = functools.partial(outer, reach, 2 * tile, width)
    several(steps, cover, waves, state, force, terms, second, third, fourth)
    if last:
        keep, give = outs
        keep[...] = state[:, pl.ds(reach + mine * tile, tile)]
        give[...] = state[:, pl.ds(reach + (1 - mine) * tile, tile)]
    else:
        slab, left, right = outs
        slab[...] = state[:, reach:far]
        left[...] = state[:, reach : reach + next_width]
        right[...] = state[:, far - next_width : far]


def finish_kernel(keep, given, out, sem):
    mine = parity()
    copies = [
        pltpu.make_async_copy(keep, out.at[mine], sem.at[0]),
        pltpu.make_async_copy(given, out.at[1 - mine], sem.at[1]),
    ]
    for copy in copies:
        copy.start()
    for copy in copies:
        copy.wait()


def per_device(perturbation, forcing, frequency, base_flow, phase_slot):
    _, _, tile, rows, lanes = perturbation.shape
    count = lax.axis_size("space")
    steps = phase_slot.shape[0]
    block = lambda *lead: jax.ShapeDtypeStruct((*lead, rows, lanes), jnp.float32)
    scratch = lambda *lead: pltpu.VMEM((*lead, rows, lanes), jnp.float32)

    rounds = [list(range(start, min(start + 2, steps))) for start in range(0, steps, 2)]
    sets = [each for each in (rounds[0], sum(rounds[1:], [])) if each]
    widths = {step: STAGES * (each[-1] - step + 1) for each in rounds for step in each}
    reach = max(widths.values())
    state_edge = widths[0] + reach - 1
    planes = 2 * (tile + reach)

    swap = [(i, i ^ 1) for i in range(count)]
    own = [(i, (i + 2 * (1 if i % 2 else -1)) % count) for i in range(count)]
    other = [(i, (i + (1 if i % 2 else -1)) % count) for i in range(count)]
    ahead = [(i, (i + 2) % count) for i in range(count)]
    behind = [(i, (i - 2) % count) for i in range(count)]
    core = [(0, 1), (1, 0)]

    base_peer = lax.ppermute(base_flow, "vec", core)
    moments = [step * TIME_STEP + part for step in range(steps) for part in (0.0, 0.5 * TIME_STEP, TIME_STEP)]

    def pack(which, keep):
        sends, copies = [], 0
        for chosen in which:
            group, start = sets[chosen], chosen == 0
            swapped = len(group) * (tile // 2) + (2 * tile if start else 0)
            edges = sum(widths[step] // 2 for step in group) + (state_edge if start else 0)
            every = sum(widths.values()) // 2 + state_edge
            sends += [block(FIELDS, swapped)] + ([block(FIELDS, every)] if start else []) + [block(FIELDS, edges)]
            copies += 2 * len(group) + (6 + steps if start else 0)
        kept = [block(FIELDS, 2 * tile), block(FIELDS, steps * tile)] if keep else []
        return pallas(
            functools.partial(pack_kernel, sets, widths, reach, which),
            "pack",
            sends + kept,
            [HBM] * 5,
            [pltpu.SMEM(phase_slot.shape, jnp.int32), pltpu.SemaphoreType.DMA((copies + (3 + steps if keep else 1),))],
        )(*in_place(phase_slot, perturbation, forcing, base_flow), base_peer)

    def exchange(packed, perms):
        return [lax.ppermute(part, "space", perm) for part, perm in zip(packed, perms)]

    def factors(which, arrived):
        group = sets[which]
        edges = sum(widths[step] // 2 for step in group)
        starts = [2 * tile, state_edge, state_edge] if which == 0 else [0, 0, 0]
        if which > 0:
            starts[1] = state_edge + sum(widths[step] // 2 for each in sets[:which] for step in each)
        sizes = (len(group) * tile // 2, edges, edges)
        parts = [part[:, at : at + size] for part, at, size in zip(arrived, starts, sizes)]
        if which == 0:
            crossed, others = [lax.ppermute(part, "vec", core) for part in parts], (0, 0, 0)
        else:
            crossed = [lax.ppermute(jnp.concatenate(parts, axis=1), "vec", core)] * 3
            others = (0, sizes[0], sizes[0] + edges)
        return pallas(
            functools.partial(terms_kernel, group, widths, group[0] * tile, (starts, others), reach),
            "terms",
            [block(TERMS, planes)] * len(group),
            [VMEM] * 7,
            [scratch(FIELDS, planes)],
            grant=2,
        )(held_base, *arrived, *crossed)

    def advance(which, operands):
        group = rounds[which]
        first, last = which == 0, which == len(rounds) - 1
        next_width = 0 if last else widths[rounds[which + 1][0]]
        if last:
            outs = [block(FIELDS, tile)] * 2
        else:
            outs = [block(FIELDS, 2 * tile), block(FIELDS, next_width), block(FIELDS, next_width)]
        if first:
            outs = [block(FIELDS, planes)] + outs
        return pallas(
            functools.partial(advance_kernel, group, widths, reach, first, last, next_width),
            "advance",
            outs,
            [VMEM] * (1 + len(operands)),
            [scratch(FIELDS, planes)] * 4,
            grant=8,
        )(waves, *operands)

    first = exchange(pack([0], False), (swap, own, other))
    *later, held_state, held_base = pack(range(1, len(sets)), True)
    (waves,) = pallas(functools.partial(waves_kernel, moments), "waves", [block(3 * steps)], [SMEM])(*in_place(frequency))
    arrived = exchange(later, (swap, other))
    first, held_state, held_base, waves = lax.optimization_barrier((first, held_state, held_base, waves))
    terms = dict(zip(sets[0], factors(0, first)))
    force, *outs = advance(0, [*[terms[step] for step in rounds[0]], held_state, *first])
    for which in range(1, len(rounds)):
        slab, left, right = outs
        left_in = lax.ppermute(right, "space", ahead)
        right_in = lax.ppermute(left, "space", behind)
        if which < len(sets):
            swap_in, other_in = after(arrived, slab)
            terms |= zip(sets[which], factors(which, [swap_in, first[1], other_in]))
        factors_here = [terms[step] for step in rounds[which]]
        begun = pallas(
            functools.partial(interior_kernel, rounds[which], reach),
            "interior",
            [block(FIELDS, 2 * tile)] * 4,
            [VMEM] * (3 + len(factors_here)),
            [scratch(FIELDS, planes)] * 4,
            grant=8,
        )(waves, *factors_here, force, slab)
        outs = advance(which, [*factors_here, force, left_in, right_in, *begun])
    keep, give = outs
    given = lax.ppermute(give, "space", swap)
    return pl.pallas_call(
        finish_kernel,
        out_shape=jax.ShapeDtypeStruct(perturbation.shape, perturbation.dtype),
        in_specs=[VMEM] * 2,
        out_specs=HBM,
        scratch_shapes=[pltpu.SemaphoreType.DMA((2,))],
        compiler_params=pltpu.CompilerParams(vmem_limit_bytes=1 << 20),
        name="finish",
    )(keep, given)


def solution(mesh):
    return jax.shard_map(
        per_device,
        mesh=mesh,
        in_specs=(
            P(("groups", "vec"), None, "space", None, None),
            P(("groups", "vec"), None, "space", None, None),
            P(("groups", "vec")),
            P("vec", None, "space", None, None),
            P(),
        ),
        out_specs=P(("groups", "vec"), None, "space", None, None),
        check_vma=False,
    )
```
